32 devices in a mesh: region: 4 (over y, core), block: 8 (over z, x).
Axes of the slice: x: 2, y: 2, z: 4, core: 2. Of those that a mesh axis runs over, the one named last changes fastest.
Arguments:
- features: bfloat16 [24576, 128], P(('region', 'block')), may hold values from -6 to 6
- grad_out: bfloat16 [24576, 128], P(('region', 'block')), may hold values from -6 to 6
- w1: bfloat16 [27, 128, 128], replicated, may hold values from -0.109375 to 0.109375
- w2: bfloat16 [27, 128, 128], replicated, may hold values from -0.109375 to 0.109375
- rulebook: int32 [27, 24576], P(None, ('region', 'block')), may hold values from 0 to 1024, as said below
- live_blocks: int32 [192], P(('region', 'block')), may hold values from 0 to 1, as said below
Outputs:
- grad_in: bfloat16 [24576, 128], P(('region', 'block'))
- grad_w1: float32 [27, 128, 128], replicated
- grad_w2: float32 [27, 128, 128], replicated
The draws below stay inside these ranges and needn't reach their ends.
Inputs may be any that keep to these rules, and one draw needn't show every extreme that they name: `rulebook`: entries index slab s's extended rows as in the reference program; the value 768 + 2 * 128 means no neighbour. Every entry of a padded row has that value; no entry points at a padded row or at a missing neighbour; offset 27 // 2 of a live row points at the row itself. An entry of row v of slab s other than 1024 lies between v - s * 768 and v - s * 768 + 2 * 128. `live_blocks`: the first 1 and the last 1 block of every slab are live; the padded blocks of a slab lie between them. Some slab has all 6 blocks live and some slab only 2.
All inputs are finite; a program needn't handle non-finite values.
Results may differ from the reference program's by a relative error of at most 0.0039.
Values may be sent and summed in bfloat16 or wider, within the bound.
A program may use at most 64 MiB of HBM per device.

```python
import jax
import jax.numpy as jnp
from jax import lax

C = 128
K = 27
BLOCK = 128
NB = 6
HB = 1
ROWS_DEV = 768
HALO = 128
SLABS = 8
VOXELS = 24576


def slab_layout(key):
    base = jax.random.fold_in(key, 4711)
    key_count, key_shift, key_keep = jax.random.split(base, 3)
    slab_count = VOXELS // ROWS_DEV
    counts = jax.random.randint(key_count, (slab_count,), 2 * HB, NB + 1)
    counts = counts.at[0].set(NB).at[1].set(2 * HB)
    block_ids = jnp.arange(NB)
    live = (block_ids[None, :] < counts[:, None] - HB) | (block_ids[None, :] >= NB - HB)
    live = live.astype(jnp.int32)
    row_live = jnp.repeat(live, BLOCK, axis=1)
    shifts = jax.random.randint(key_shift, (K, slab_count, ROWS_DEV), -HALO, HALO + 1)
    center = (jnp.arange(K) == K // 2)[:, None, None]
    shifts = jnp.where(center, 0, shifts)
    keeper = (jax.random.randint(key_keep, (K, slab_count, ROWS_DEV), 0, 4) > 0) | center
    target = jnp.arange(ROWS_DEV)[None, None, :] + shifts
    position = (jnp.arange(slab_count) % SLABS)[None, :, None]
    inside = ((target >= 0) | (position > 0)) & ((target < ROWS_DEV) | (position < SLABS - 1))
    clipped = jnp.clip(target, 0, ROWS_DEV - 1)
    target_live = jnp.take_along_axis(jnp.broadcast_to(row_live[None], (K, slab_count, ROWS_DEV)), clipped, axis=2)
    target_live = jnp.where((target >= 0) & (target < ROWS_DEV), target_live, 1)
    usable = keeper & inside & (target_live == 1) & (row_live[None] == 1)
    rule_table = jnp.where(usable, target + HALO, ROWS_DEV + 2 * HALO).astype(jnp.int32)
    return (rule_table.reshape(K, slab_count * ROWS_DEV), live.reshape(slab_count * NB))


def draw_rulebook(key, part):
    return slab_layout(key)[0]


def draw_live_blocks(key, part):
    return slab_layout(key)[1]


def level_of(key, dims, cuts, least, largest):
    def one(dim, parts):
        heights = jax.random.uniform(jax.random.fold_in(jax.random.fold_in(key, 6), dim), (parts,), jnp.float32, least / len(cuts), largest / len(cuts))
        return jnp.repeat(jnp.exp(heights), dims[dim] // parts).reshape((-1,) + (1,) * (len(dims) - dim - 1))

    factor_of = one(*cuts[0])
    for cut in cuts[1:]:
        factor_of = factor_of * one(*cut)
    return factor_of


def scatter_about(stream_key, dims, deviation, reach, cuts=(), held_as=jnp.bfloat16):
    drawn = deviation * jax.random.normal(stream_key, dims, jnp.float32)
    if cuts:
        drawn = drawn * level_of(stream_key, dims, cuts, -0.22, 0.18)
    return jnp.clip(drawn, -reach, reach).astype(held_as)


def setup_inputs(seed: int = 0) -> dict:
    key_of = jax.random.split(jax.random.key(seed), 7)
    return {
        "features": scatter_about(key_of[0], (VOXELS, C), 1.0, 6.0, ((0, 32),)),
        "grad_out": scatter_about(key_of[1], (VOXELS, C), 1.0, 6.0, ((0, 32),)),
        "w1": scatter_about(key_of[2], (K, C, C), (K * C) ** -0.5, 0.109375),
        "w2": scatter_about(key_of[3], (K, C, C), (K * C) ** -0.5, 0.109375),
        "rulebook": draw_rulebook(jax.random.fold_in(key_of[6], 71), 0),
        "live_blocks": draw_live_blocks(jax.random.fold_in(key_of[6], 71), 0),
    }


def dsilu(hidden):
    sigma = jax.nn.sigmoid(hidden)
    return sigma * (1.0 + hidden * (1.0 - sigma))

def extend(values):
    slab_count = values.shape[0]
    chans = values.shape[2]
    position = jnp.arange(slab_count) % SLABS
    rim_zeros = jnp.zeros((1, HALO, chans), values.dtype)
    before = jnp.concatenate([rim_zeros, values[:-1, ROWS_DEV - HALO:]], 0)
    before = jnp.where((position > 0)[:, None, None], before, jnp.zeros_like(before))
    after = jnp.concatenate([values[1:, :HALO], rim_zeros], 0)
    after = jnp.where((position < SLABS - 1)[:, None, None], after, jnp.zeros_like(after))
    blank = jnp.zeros((slab_count, 1, chans), values.dtype)
    return jnp.concatenate([before, values, after, blank], 1)

def gather_rows(extended, lookup):
    return jax.vmap(lambda source, picks: source[picks])(extended, lookup)

def fold_back(scattered):
    slab_count = scattered.shape[0]
    chans = scattered.shape[2]
    position = jnp.arange(slab_count) % SLABS
    own_rows = scattered[:, HALO:HALO + ROWS_DEV]
    lower_rim = scattered[:, :HALO]
    upper_rim = scattered[:, HALO + ROWS_DEV:2 * HALO + ROWS_DEV]
    rim_zeros = jnp.zeros((1, HALO, chans), scattered.dtype)
    from_above = jnp.concatenate([lower_rim[1:], rim_zeros], 0)
    from_above = jnp.where((position < SLABS - 1)[:, None, None], from_above, jnp.zeros_like(from_above))
    from_below = jnp.concatenate([rim_zeros, upper_rim[:-1]], 0)
    from_below = jnp.where((position > 0)[:, None, None], from_below, jnp.zeros_like(from_below))
    own_rows = own_rows.at[:, :HALO].add(from_below)
    own_rows = own_rows.at[:, ROWS_DEV - HALO:].add(from_above)
    return own_rows

def reference(features, grad_out, w1, w2, rulebook, live_blocks):
    slab_count = VOXELS // ROWS_DEV
    rule_table = rulebook.reshape(K, slab_count, ROWS_DEV)
    ext_feat = extend(features.reshape(slab_count, ROWS_DEV, C))

    def forward(running, pair):
        weight, lookup = pair
        picked = gather_rows(ext_feat, lookup).reshape(-1, C)
        return (running + jnp.dot(picked, weight, preferred_element_type=jnp.float32), None)
    hidden, _ = lax.scan(forward, jnp.zeros((VOXELS, C), jnp.float32), (w1, rule_table))
    act = jax.nn.silu(hidden).astype(jnp.bfloat16)
    ext_act = extend(act.reshape(slab_count, ROWS_DEV, C))
    scale = jnp.sqrt(jnp.float32(VOXELS))

    def kernel_grad(extended, right_side):

        def step(running, lookup):
            picked = gather_rows(extended, lookup).reshape(-1, C)
            return (running, jnp.dot(picked.T, right_side, preferred_element_type=jnp.float32))
        _, grads = lax.scan(step, jnp.zeros((), jnp.float32), rule_table)
        return grads / scale

    def scatter_back(source, weights):
        start = jnp.zeros((slab_count, ROWS_DEV + 2 * HALO + 1, C), jnp.float32)

        def step(running, pair):
            weight, lookup = pair
            spread = jnp.dot(source, weight.T, preferred_element_type=jnp.float32).reshape(slab_count, ROWS_DEV, C)
            added = jax.vmap(lambda target, picks, terms: target.at[picks].add(terms))(running, lookup, spread)
            return (added, None)
        scattered, _ = lax.scan(step, start, (weights, rule_table))
        return fold_back(scattered).reshape(VOXELS, C)
    grad_w2 = kernel_grad(ext_act, grad_out)
    grad_act = scatter_back(grad_out, w2)
    grad_hidden = (grad_act * dsilu(hidden)).astype(jnp.bfloat16)
    grad_w1 = kernel_grad(ext_feat, grad_hidden)
    grad_feat = scatter_back(grad_hidden, w1)
    live = jnp.repeat(live_blocks, BLOCK).astype(jnp.float32)[:, None]
    grad_in = (live * (grad_out.astype(jnp.float32) + grad_feat)).astype(jnp.bfloat16)
    return (grad_in, grad_w1, grad_w2)
```

```python
import functools

import jax
import jax.numpy as jnp
from jax import lax
from jax.experimental import pallas as pl
from jax.experimental.pallas import tpu as pltpu
from jax.sharding import PartitionSpec as P

BLOCK = 128
HALO = 128
NOWHERE = 4.0 * BLOCK
MESH = pl.DeviceIdType.MESH
F32 = jnp.float32
BF16 = jnp.bfloat16


def slab_kernel(
    region, length, scale,
    feat, gout, w1, w2, rule, live,
    grad_in, out1, out2,
    w1v, w2v, w1c, w2c, w1t, ft, gt, ht, act, near, picks, spread, hidden,
    fin, gin, rin, hout, hin, load, send, recv,
    partial, own, mine, rest, got1, got2, got3,
    send_there, recv_there, send_back, recv_back,
):
    rows, chans = feat.shape
    offsets = w1.shape[0]
    blocks = rows // BLOCK
    pairs = blocks // 2
    ext_blocks = blocks + 2
    wide = offsets * chans
    part_rows = partial.shape[1]
    me = lax.axis_index("block")
    left, right = me - 1, me + 1
    has_left, has_right = me > 0, me < length - 1

    loads = [pltpu.make_async_copy(w1, w1v, load.at[0]), pltpu.make_async_copy(w2, w2v, load.at[1])]
    for copy in loads:
        copy.start()

    def copies(i, low, high, arrived):
        down = pltpu.make_async_remote_copy(
            src_ref=low, dst_ref=arrived.at[1], send_sem=send.at[i, 0], recv_sem=recv.at[i, 0],
            device_id={"block": left}, device_id_type=MESH)
        up = pltpu.make_async_remote_copy(
            src_ref=high, dst_ref=arrived.at[0], send_sem=send.at[i, 1], recv_sem=recv.at[i, 1],
            device_id={"block": right}, device_id_type=MESH)
        return down, up

    def start(pair):
        down, up = pair
        pl.when(has_left)(down.start)
        pl.when(has_right)(up.start)

    def finish(pair):
        down, up = pair

        @pl.when(has_left)
        def _():
            down.wait_send()
            up.wait_recv()

        @pl.when(has_right)
        def _():
            up.wait_send()
            down.wait_recv()

    stages, peers = sum_stages(
        region, length, scale, partial, (out1, out2), own, mine, rest, got1, got2, got3,
        send_there, recv_there, send_back, recv_back)
    barrier = pltpu.get_barrier_semaphore()
    for peer in peers:
        pl.semaphore_signal(barrier, inc=1, device_id=peer, device_id_type=MESH)

    @pl.when(has_left)
    def _():
        pl.semaphore_signal(barrier, inc=1, device_id={"block": left}, device_id_type=MESH)

    @pl.when(has_right)
    def _():
        pl.semaphore_signal(barrier, inc=1, device_id={"block": right}, device_id_type=MESH)

    def entry(e):
        return slice(e * BLOCK, (e + 1) * BLOCK)

    def reach(rule_part, e):
        value = (rule_part - e * BLOCK).astype(F32)
        return jnp.where(rule_part == rows + 2 * HALO, NOWHERE, value)

    for e in range(1, blocks + 1):
        ft[:, entry(e)] = feat[entry(e - 1)].T
        gt[:, entry(e)] = gout[entry(e - 1)].T
        near[:, entry(e)] = reach(rule[:, entry(e - 1)], e)

    pl.semaphore_wait(
        barrier, len(peers) + has_left.astype(jnp.int32) + has_right.astype(jnp.int32))
    first, last = pl.ds(0, HALO), pl.ds(rows - HALO, HALO)
    halo_copies = [
        copies(0, feat.at[first], feat.at[last], fin),
        copies(1, rule.at[:, first], rule.at[:, last], rin),
        copies(2, gout.at[first], gout.at[last], gin),
    ]
    hidden_copies = copies(3, hout.at[0], hout.at[1], hin)
    for pair in halo_copies:
        start(pair)

    edge = jnp.zeros((HALO, chans), BF16)
    none = jnp.full((offsets, HALO), rows + 2 * HALO, jnp.int32)
    for side, missing in ((0, jnp.logical_not(has_left)), (1, jnp.logical_not(has_right))):
        @pl.when(missing)
        def _(side=side):
            fin[side] = edge
            gin[side] = edge
            hin[side] = edge
            rin[side] = none

    for copy in loads:
        copy.wait()
    for k in range(offsets):
        w1c[:, entry(k)] = w1v[k]
        w1t[:, entry(k)] = w1v[k].T
        w2c[:, entry(k)] = w2v[k]

    for pair in halo_copies:
        finish(pair)
    for side, e, seen in ((0, 0, blocks), (1, blocks + 1, 1)):
        ft[:, entry(e)] = fin[side].T
        gt[:, entry(e)] = gin[side].T
        near[:, entry(e)] = reach(rin[side], seen)

    one, zero = jnp.ones((BLOCK, BLOCK), BF16), jnp.zeros((BLOCK, BLOCK), BF16)

    def steps(dim):
        base = lax.broadcasted_iota(jnp.int32, (BLOCK, BLOCK), dim)
        return [(base + d * BLOCK).astype(BF16) for d in (-1, 0, 1)]

    def row_of(k, begin):
        value = near[k:k + 1, pl.ds(pl.multiple_of(begin, BLOCK), BLOCK)].astype(BF16)
        return jnp.broadcast_to(value, (BLOCK, BLOCK))

    def gather(source, out):
        at = steps(0)

        @pl.loop(0, pairs)
        def _(b):
            begin = pl.multiple_of(b * 2 * BLOCK, BLOCK)
            window = source[:, pl.ds(begin, 4 * BLOCK)]
            for k in range(offsets):
                sides = [row_of(k, begin + (j + 1) * BLOCK) for j in range(2)]
                chosen = jnp.concatenate([
                    jnp.concatenate([
                        jnp.where(sides[j] == at[i - j], one, zero) if 0 <= i - j < 3 else zero
                        for i in range(4)], 0)
                    for j in range(2)], 1)
                out[entry(k), pl.ds(begin, 2 * BLOCK)] = jnp.dot(
                    window, chosen, preferred_element_type=F32).astype(BF16)

    def scatter(source, out):
        at = steps(1)

        @pl.loop(0, pairs)
        def _(b):
            begin = pl.multiple_of(b * 2 * BLOCK, BLOCK)
            window = source[:, pl.ds(begin, 4 * BLOCK)]
            for k in range(offsets):
                sides = [row_of(k, begin + i * BLOCK).T for i in range(4)]
                chosen = jnp.concatenate([
                    jnp.concatenate([
                        jnp.where(sides[i] == at[j - i + 2], one, zero) if 0 <= j - i + 2 < 3 else zero
                        for j in range(2)], 1)
                    for i in range(4)], 0)
                out[entry(k), pl.ds(begin, 2 * BLOCK)] = jnp.dot(
                    window, chosen, preferred_element_type=F32).astype(BF16)

    tail = part_rows - wide
    if tail:
        for i in range(2):
            partial[i, pl.ds(wide, tail)] = jnp.zeros((tail, chans), F32)

    parts = 3 if offsets % 3 == 0 else 1
    step = offsets // parts

    gather(ft, picks)
    value = jnp.dot(w1t[...], picks[...], preferred_element_type=F32)
    hidden[...] = value
    act[...] = (value / (1.0 + jnp.exp(-value))).astype(BF16)

    scatter(gt, spread)
    for p in range(parts):
        got = lax.dot_general(
            act[...], spread[pl.ds(p * step * chans, step * chans)], (((1,), (1,)), ((), ())),
            preferred_element_type=F32)
        for k in range(step):
            partial[1, entry(p * step + k)] = got[:, entry(k)]
    ready, later = stages(1), stages(0)
    next(ready)

    grad_act = jnp.dot(w2c[...], spread[...], preferred_element_type=F32)
    value = hidden[...]
    sigma = 1.0 / (1.0 + jnp.exp(-value))
    slope = sigma * (1.0 + value * (1.0 - sigma))
    ht[:, pl.ds(HALO, rows)] = (grad_act * slope).astype(BF16)
    hout[0] = ht[:, entry(1)]
    hout[1] = ht[:, entry(blocks)]
    start(hidden_copies)
    next(ready)

    turned = jnp.concatenate([ht[:, entry(e)].T for e in range(1, blocks + 1)], 0)
    for p in range(parts):
        at = pl.ds(p * step * chans, step * chans)
        partial[0, at] = jnp.dot(picks[at], turned, preferred_element_type=F32)
    next(later)
    next(ready)

    finish(hidden_copies)
    ht[:, entry(0)] = hin[0]
    ht[:, entry(blocks + 1)] = hin[1]
    scatter(ht, spread)
    next(later)
    grad_feat = jnp.dot(w1c[...], spread[...], preferred_element_type=F32)
    for b in range(blocks):
        keep = live[b].astype(F32)
        grad_in[entry(b)] = (
            keep * (gout[entry(b)].astype(F32) + grad_feat[:, entry(b)].T)).astype(BF16)
    next(ready)
    next(later)
    for _ in range(3):
        next(ready)
        next(later)
    next(later)


def slab_step(features, grad_out, w1, w2, rulebook, live_blocks, part_rows, scale):
    region, block = lax.axis_size("region"), lax.axis_size("block")
    planes, depth = region // 2 * 2, block // 2
    half = part_rows // 2
    quarter = half // planes
    piece = quarter // depth
    count = planes + depth - 1
    rows, chans = features.shape
    offsets = w1.shape[0]
    ext = rows + 2 * HALO
    wide = offsets * chans
    vmem = pl.BlockSpec(memory_space=pltpu.VMEM)
    hbm = pl.BlockSpec(memory_space=pl.ANY)
    return pl.pallas_call(
        functools.partial(slab_kernel, region, block, scale),
        out_shape=(
            jax.ShapeDtypeStruct((rows, chans), BF16),
            jax.ShapeDtypeStruct((part_rows, chans), BF16),
            jax.ShapeDtypeStruct((part_rows, chans), BF16),
        ),
        in_specs=[vmem, vmem, hbm, hbm, vmem, pl.BlockSpec(memory_space=pltpu.SMEM)],
        out_specs=(vmem, vmem, vmem),
        scratch_shapes=[
            pltpu.VMEM((offsets, chans, chans), BF16),
            pltpu.VMEM((offsets, chans, chans), BF16),
            pltpu.VMEM((chans, wide), BF16),
            pltpu.VMEM((chans, wide), BF16),
            pltpu.VMEM((chans, wide), BF16),
            pltpu.VMEM((chans, ext), BF16),
            pltpu.VMEM((chans, ext), BF16),
            pltpu.VMEM((chans, ext), BF16),
            pltpu.VMEM((chans, rows), BF16),
            pltpu.VMEM((offsets, ext), F32),
            pltpu.VMEM((wide, rows), BF16),
            pltpu.VMEM((wide, rows), BF16),
            pltpu.VMEM((chans, rows), F32),
            pltpu.VMEM((2, HALO, chans), BF16),
            pltpu.VMEM((2, HALO, chans), BF16),
            pltpu.VMEM((2, offsets, HALO), jnp.int32),
            pltpu.VMEM((2, chans, HALO), BF16),
            pltpu.VMEM((2, chans, HALO), BF16),
            pltpu.SemaphoreType.DMA((2,)),
            pltpu.SemaphoreType.DMA((4, 2)),
            pltpu.SemaphoreType.DMA((4, 2)),
            pltpu.VMEM((2, part_rows, chans), F32),
            pltpu.VMEM((2, quarter, chans), F32),
            pltpu.VMEM((2, half, chans), BF16),
            pltpu.VMEM((2, quarter, chans), BF16),
            pltpu.VMEM((2, half, chans), F32),
            pltpu.VMEM((2, planes - 1, quarter, chans), BF16),
            pltpu.VMEM((2, depth - 1, piece, chans), BF16),
        ] + [pltpu.SemaphoreType.DMA((2, count))] * 4,
        compiler_params=pltpu.CompilerParams(
            collective_id=0, has_side_effects=True, vmem_limit_bytes=64000000),
    )(features, grad_out, w1, w2, rulebook, live_blocks)


def sum_stages(region, block, scale, part, out, own, mine, rest, got1, got2, got3,
               send_there, recv_there, send_back, recv_back):
    half = part.shape[1] // 2
    planes, depth = region // 2 * 2, block // 2
    quarter = half // planes
    piece = quarter // depth
    r, b = lax.axis_index("region"), lax.axis_index("block")
    c, y, x, z = lax.rem(r, 2), r // 2, lax.rem(b, 2), b // 2
    p = y * 2 + x

    def device(core, plane, deep):
        return {"region": plane // 2 * 2 + core, "block": deep * 2 + lax.rem(plane, 2)}

    partner = device(1 - c, p, z)
    plane_peers = [device(c, lax.rem(p + d, planes), z) for d in range(1, planes)]
    deep_peers = [device(c, p, lax.rem(z + d, depth)) for d in range(1, depth)]

    def at(index, size):
        return pl.ds(pl.multiple_of(index * size, 16), size)

    def remote(src, dst, sems, i, n, peer):
        copy = pltpu.make_async_remote_copy(
            src_ref=src, dst_ref=dst, send_sem=sems[0].at[i, n], recv_sem=sems[1].at[i, n],
            device_id=peer, device_id_type=MESH)
        copy.start()
        return copy

    there = (send_there, recv_there)
    back = (send_back, recv_back)

    def stages(i):
        first = remote(part.at[i, at(1 - c, half)], got1.at[i], there, i, 0, partner)
        yield
        first.wait()
        mine[i] = (part[i, at(c, half)] + got1[i]).astype(BF16)
        second = [remote(mine.at[i, at(lax.rem(p + d, planes), quarter)], got2.at[i, d - 1],
                         there, i, d, plane_peers[d - 1]) for d in range(1, planes)]
        yield
        value = part[i, at(c * planes + p, quarter)] + got1[i, at(p, quarter)]
        for d in range(1, planes):
            second[d - 1].wait()
            value = value + got2[i, d - 1].astype(F32)
        own[i] = value
        rest[i] = value.astype(BF16)
        third = [remote(rest.at[i, at(lax.rem(z + d, depth), piece)], got3.at[i, d - 1],
                        there, i, planes - 1 + d, deep_peers[d - 1]) for d in range(1, depth)]
        yield
        value = own[i, at(z, piece)]
        for d in range(1, depth):
            third[d - 1].wait()
            value = value + got3[i, d - 1].astype(F32)
        place = at((c * planes + p) * depth + z, piece)
        out[i][place] = (value / scale).astype(BF16)
        for where, peers, base in (
            (place, deep_peers, planes),
            (at(c * planes + p, quarter), plane_peers, 1),
            (at(c, half), [partner], 0),
        ):
            moved = [remote(out[i].at[where], out[i].at[where], back, i, base + n, peer)
                     for n, peer in enumerate(peers)]
            yield
            for copy in moved:
                copy.wait()
        yield

    return stages, [partner] + plane_peers + deep_peers


def on_device(features, grad_out, w1, w2, rulebook, live_blocks):
    offsets, chans = w1.shape[0], w1.shape[1]
    devices = lax.axis_size("region") * lax.axis_size("block")
    step = 16 * devices
    part_rows = (offsets * chans + step - 1) // step * step
    scale = float(features.shape[0] * devices) ** 0.5
    grad_in, *both = slab_step(
        features, grad_out, w1, w2, rulebook, live_blocks, part_rows, scale)
    grad_w1, grad_w2 = (
        part[:offsets * chans].astype(F32).reshape(offsets, chans, chans) for part in both)
    return (grad_in, grad_w1, grad_w2)


def solution(mesh):
    return jax.shard_map(
        on_device,
        mesh=mesh,
        in_specs=(
            P(("region", "block"), None),
            P(("region", "block"), None),
            P(),
            P(),
            P(None, ("region", "block")),
            P(("region", "block")),
        ),
        out_specs=(P(("region", "block"), None), P(), P()),
        check_vma=False,
    )
```

```python
import functools

import jax
import jax.numpy as jnp
from jax import lax
from jax.experimental import pallas as pl
from jax.experimental.pallas import tpu as pltpu
from jax.sharding import PartitionSpec as P

BLOCK = 128
HALO = 128
NOWHERE = 4.0 * BLOCK
PARTS = 3
MESH = pl.DeviceIdType.MESH
F32 = jnp.float32
BF16 = jnp.bfloat16


def slab_kernel(
    region, length, scale, cuts,
    feat, gout, w1, w2, rule, live,
    grad_in, out1, out2,
    w1v, w2v, w1c, w2c, w1t, ft, gt, ht, act, near, picks, spread, hidden,
    fin, gin, rin, hout, hin, load, send, recv, store,
    partial, total, own, mine, rest, got1, got2, got3,
    send_there, recv_there, send_back, recv_back,
):
    rows, chans = feat.shape
    offsets = w1.shape[0]
    blocks = rows // BLOCK
    pairs = blocks // 2
    ext_blocks = blocks + 2
    wide = offsets * chans
    part_rows = partial.shape[1]
    me = lax.axis_index("block")
    left, right = me - 1, me + 1
    has_left, has_right = me > 0, me < length - 1

    loads = [pltpu.make_async_copy(w1, w1v, load.at[0]), pltpu.make_async_copy(w2, w2v, load.at[1])]
    for copy in loads:
        copy.start()

    def copies(i, low, high, arrived):
        down = pltpu.make_async_remote_copy(
            src_ref=low, dst_ref=arrived.at[1], send_sem=send.at[i, 0], recv_sem=recv.at[i, 0],
            device_id={"block": left}, device_id_type=MESH)
        up = pltpu.make_async_remote_copy(
            src_ref=high, dst_ref=arrived.at[0], send_sem=send.at[i, 1], recv_sem=recv.at[i, 1],
            device_id={"block": right}, device_id_type=MESH)
        return down, up

    def start(pair):
        down, up = pair
        pl.when(has_left)(down.start)
        pl.when(has_right)(up.start)

    def finish(pair):
        down, up = pair

        @pl.when(has_left)
        def _():
            down.wait_send()
            up.wait_recv()

        @pl.when(has_right)
        def _():
            up.wait_send()
            down.wait_recv()

    stages, peers = sum_stages(
        region, length, scale, cuts, wide, partial, total, (out1, out2), store, own, mine, rest, got1, got2, got3,
        send_there, recv_there, send_back, recv_back)
    barrier = pltpu.get_barrier_semaphore()
    for peer in peers:
        pl.semaphore_signal(barrier, inc=1, device_id=peer, device_id_type=MESH)

    @pl.when(has_left)
    def _():
        pl.semaphore_signal(barrier, inc=1, device_id={"block": left}, device_id_type=MESH)

    @pl.when(has_right)
    def _():
        pl.semaphore_signal(barrier, inc=1, device_id={"block": right}, device_id_type=MESH)

    def entry(e):
        return slice(e * BLOCK, (e + 1) * BLOCK)

    def reach(rule_part, e):
        value = (rule_part - e * BLOCK).astype(F32)
        return jnp.where(rule_part == rows + 2 * HALO, NOWHERE, value)

    for e in range(1, blocks + 1):
        ft[:, entry(e)] = feat[entry(e - 1)].T
        gt[:, entry(e)] = gout[entry(e - 1)].T
        near[:, entry(e)] = reach(rule[:, entry(e - 1)], e)

    for copy in loads:
        copy.wait()
    for k in range(offsets):
        w1c[:, entry(k)] = w1v[k]
        w1t[:, entry(k)] = w1v[k].T
        w2c[:, entry(k)] = w2v[k]

    one, zero = jnp.ones((BLOCK, BLOCK), BF16), jnp.zeros((BLOCK, BLOCK), BF16)

    def steps(dim):
        base = lax.broadcasted_iota(jnp.int32, (BLOCK, BLOCK), dim)
        return [(base + d * BLOCK).astype(BF16) for d in (-1, 0, 1)]

    def row_of(k, begin):
        value = near[k:k + 1, pl.ds(pl.multiple_of(begin, BLOCK), BLOCK)].astype(BF16)
        return jnp.broadcast_to(value, (BLOCK, BLOCK))

    def gather(source, out, b, ks):
        at = steps(0)
        begin = pl.multiple_of(b * 2 * BLOCK, BLOCK)
        window = source[:, pl.ds(begin, 4 * BLOCK)]
        for k in ks:
            sides = [row_of(k, begin + (j + 1) * BLOCK) for j in range(2)]
            chosen = jnp.concatenate([
                jnp.concatenate([
                    jnp.where(sides[j] == at[i - j], one, zero) if 0 <= i - j < 3 else zero
                    for i in range(4)], 0)
                for j in range(2)], 1)
            out[entry(k), pl.ds(begin, 2 * BLOCK)] = jnp.dot(
                window, chosen, preferred_element_type=F32).astype(BF16)

    def scatter(source, out, b, ks):
        at = steps(1)
        begin = pl.multiple_of(b * 2 * BLOCK, BLOCK)
        window = source[:, pl.ds(begin, 4 * BLOCK)]
        for k in ks:
            sides = [row_of(k, begin + i * BLOCK).T for i in range(4)]
            chosen = jnp.concatenate([
                jnp.concatenate([
                    jnp.where(sides[i] == at[j - i + 2], one, zero) if 0 <= j - i + 2 < 3 else zero
                    for j in range(2)], 1)
                for i in range(4)], 0)
            out[entry(k), pl.ds(begin, 2 * BLOCK)] = jnp.dot(
                window, chosen, preferred_element_type=F32).astype(BF16)

    inner, outer = range(1, pairs - 1), (0, pairs - 1)
    every = range(offsets)

    def over(pair_blocks, job, source, out, ks):
        first, stride = pair_blocks[0], pair_blocks[-1] - pair_blocks[0]

        @pl.loop(0, len(pair_blocks))
        def _(n):
            job(source, out, first + n * stride // max(1, len(pair_blocks) - 1), ks)

    for b in inner:
        gather(ft, picks, b, every)

    pl.semaphore_wait(
        barrier, len(peers) + has_left.astype(jnp.int32) + has_right.astype(jnp.int32))
    first, last = pl.ds(0, HALO), pl.ds(rows - HALO, HALO)
    halo_copies = [
        copies(0, feat.at[first], feat.at[last], fin),
        copies(1, rule.at[:, first], rule.at[:, last], rin),
        copies(2, gout.at[first], gout.at[last], gin),
    ]
    hidden_copies = copies(3, hout.at[0], hout.at[1], hin)
    for pair in halo_copies:
        start(pair)

    edge = jnp.zeros((HALO, chans), BF16)
    none = jnp.full((offsets, HALO), rows + 2 * HALO, jnp.int32)
    for side, missing in ((0, jnp.logical_not(has_left)), (1, jnp.logical_not(has_right))):
        @pl.when(missing)
        def _(side=side):
            fin[side] = edge
            gin[side] = edge
            hin[side] = edge
            rin[side] = none

    for b in inner:
        scatter(gt, spread, b, every)

    for pair in halo_copies:
        finish(pair)
    for side, e, seen in ((0, 0, blocks), (1, blocks + 1, 1)):
        ft[:, entry(e)] = fin[side].T
        gt[:, entry(e)] = gin[side].T
        near[:, entry(e)] = reach(rin[side], seen)

    tail = part_rows - wide
    if tail:
        for i in range(2):
            partial[i, pl.ds(wide, tail)] = jnp.zeros((tail, chans), F32)

    count = len(cuts) - 1
    sums = [[stages(i, n) for n in range(count)] for i in range(2)]

    def poke(*which):
        for i, n in which:
            if 0 <= n < count:
                next(sums[i][n])

    spans = [range(min(offsets, lo // chans), min(offsets, hi // chans))
             for lo, hi in zip(cuts[:-1], cuts[1:])]

    over(outer, gather, ft, picks, every)
    value = jnp.dot(w1t[...], picks[...], preferred_element_type=F32)
    hidden[...] = value
    act[...] = (value / (1.0 + jnp.exp(-value))).astype(BF16)

    for n, ks in enumerate(spans):
        over(outer, scatter, gt, spread, ks)
        got = lax.dot_general(
            act[...], spread[pl.ds(ks[0] * chans, len(ks) * chans)], (((1,), (1,)), ((), ())),
            preferred_element_type=F32)
        for k in ks:
            partial[1, entry(k)] = got[:, entry(k - ks[0])]
        poke((1, n - 1), (1, n))

    grad_act = jnp.dot(w2c[...], spread[...], preferred_element_type=F32)
    value = hidden[...]
    sigma = 1.0 / (1.0 + jnp.exp(-value))
    slope = sigma * (1.0 + value * (1.0 - sigma))
    ht[:, pl.ds(HALO, rows)] = (grad_act * slope).astype(BF16)
    hout[0] = ht[:, entry(1)]
    hout[1] = ht[:, entry(blocks)]
    start(hidden_copies)
    poke((1, count - 1), (1, 0))

    turned = jnp.concatenate([ht[:, entry(e)].T for e in range(1, blocks + 1)], 0)
    for n, ks in enumerate(spans):
        at = pl.ds(ks[0] * chans, len(ks) * chans)
        partial[0, at] = jnp.dot(picks[at], turned, preferred_element_type=F32)
        poke((0, n), (0, n - 1))
        if n > 0:
            poke((1, n))

    for b in inner:
        scatter(ht, spread, b, every)
    poke((0, count - 1), (1, 0), (0, 0))
    finish(hidden_copies)
    ht[:, entry(0)] = hin[0]
    ht[:, entry(blocks + 1)] = hin[1]
    scatter(ht, spread, outer[0], every)
    poke((1, 1), (0, 1), (1, 0))
    scatter(ht, spread, outer[1], every)
    poke((1, 2), (0, 2), (1, 1), (0, 0))
    grad_feat = jnp.dot(w1c[...], spread[...], preferred_element_type=F32)
    for b in range(blocks):
        keep = live[b].astype(F32)
        grad_in[entry(b)] = (
            keep * (gout[entry(b)].astype(F32) + grad_feat[:, entry(b)].T)).astype(BF16)
    left_over = [sums[i][n] for n in range(count) for i in (1, 0)]
    stores = []
    while left_over:
        going = []
        for one_sum in left_over:
            copy = next(one_sum)
            if copy is None:
                going.append(one_sum)
            else:
                stores.append(copy)
        left_over = going
    for copy in stores:
        copy.wait()


def slab_step(features, grad_out, w1, w2, rulebook, live_blocks, cuts, scale):
    region, block = lax.axis_size("region"), lax.axis_size("block")
    planes, depth = region // 2 * 2, block // 2
    part_rows = cuts[-1]
    half = part_rows // 2
    quarter = half // planes
    piece = quarter // depth
    count = planes + depth - 1
    rows, chans = features.shape
    offsets = w1.shape[0]
    ext = rows + 2 * HALO
    wide = offsets * chans
    vmem = pl.BlockSpec(memory_space=pltpu.VMEM)
    hbm = pl.BlockSpec(memory_space=pl.ANY)
    return pl.pallas_call(
        functools.partial(slab_kernel, region, block, scale, cuts),
        out_shape=(
            jax.ShapeDtypeStruct((rows, chans), BF16),
            jax.ShapeDtypeStruct((wide, chans), BF16),
            jax.ShapeDtypeStruct((wide, chans), BF16),
        ),
        in_specs=[vmem, vmem, hbm, hbm, vmem, pl.BlockSpec(memory_space=pltpu.SMEM)],
        out_specs=(vmem, hbm, hbm),
        scratch_shapes=[
            pltpu.VMEM((offsets, chans, chans), BF16),
            pltpu.VMEM((offsets, chans, chans), BF16),
            pltpu.VMEM((chans, wide), BF16),
            pltpu.VMEM((chans, wide), BF16),
            pltpu.VMEM((chans, wide), BF16),
            pltpu.VMEM((chans, ext), BF16),
            pltpu.VMEM((chans, ext), BF16),
            pltpu.VMEM((chans, ext), BF16),
            pltpu.VMEM((chans, rows), BF16),
            pltpu.VMEM((offsets, ext), F32),
            pltpu.VMEM((wide, rows), BF16),
            pltpu.VMEM((wide, rows), BF16),
            pltpu.VMEM((chans, rows), F32),
            pltpu.VMEM((2, HALO, chans), BF16),
            pltpu.VMEM((2, HALO, chans), BF16),
            pltpu.VMEM((2, offsets, HALO), jnp.int32),
            pltpu.VMEM((2, chans, HALO), BF16),
            pltpu.VMEM((2, chans, HALO), BF16),
            pltpu.SemaphoreType.DMA((2,)),
            pltpu.SemaphoreType.DMA((4, 2)),
            pltpu.SemaphoreType.DMA((4, 2)),
            pltpu.SemaphoreType.DMA((2, len(cuts) - 1)),
            pltpu.VMEM((2, part_rows, chans), F32),
            pltpu.VMEM((2, part_rows, chans), BF16),
            pltpu.VMEM((2, quarter, chans), F32),
            pltpu.VMEM((2, half, chans), BF16),
            pltpu.VMEM((2, quarter, chans), BF16),
            pltpu.VMEM((2, half, chans), F32),
            pltpu.VMEM((2, planes - 1, quarter, chans), BF16),
            pltpu.VMEM((2, depth - 1, piece, chans), BF16),
        ] + [pltpu.SemaphoreType.DMA((2, len(cuts) - 1, count))] * 4,
        compiler_params=pltpu.CompilerParams(
            collective_id=0, has_side_effects=True, vmem_limit_bytes=64000000),
    )(features, grad_out, w1, w2, rulebook, live_blocks)


def sum_stages(region, block, scale, cuts, wide, part, total, outs, store, own, mine, rest,
               got1, got2, got3, send_there, recv_there, send_back, recv_back):
    planes, depth = region // 2 * 2, block // 2
    r, b = lax.axis_index("region"), lax.axis_index("block")
    c, y, x, z = lax.rem(r, 2), r // 2, lax.rem(b, 2), b // 2
    p = y * 2 + x

    def device(core, plane, deep):
        return {"region": plane // 2 * 2 + core, "block": deep * 2 + lax.rem(plane, 2)}

    partner = device(1 - c, p, z)
    plane_peers = [device(c, lax.rem(p + d, planes), z) for d in range(1, planes)]
    deep_peers = [device(c, p, lax.rem(z + d, depth)) for d in range(1, depth)]

    def stages(i, n):
        base, size = cuts[n], cuts[n + 1] - cuts[n]
        half = size // 2
        quarter = half // planes
        piece = quarter // depth
        base1 = base // 2
        base2 = base1 // planes
        base3 = base2 // depth

        def at(start, index, count):
            return pl.ds(pl.multiple_of(start + index * count, 16), count)

        def remote(src, dst, sems, m, peer):
            copy = pltpu.make_async_remote_copy(
                src_ref=src, dst_ref=dst, send_sem=sems[0].at[i, n, m],
                recv_sem=sems[1].at[i, n, m], device_id=peer, device_id_type=MESH)
            copy.start()
            return copy

        there = (send_there, recv_there)
        back = (send_back, recv_back)
        halves, quarters, pieces = pl.ds(base1, half), pl.ds(base2, quarter), pl.ds(base3, piece)

        first = remote(part.at[i, at(base, 1 - c, half)], got1.at[i, halves], there, 0, partner)
        yield
        first.wait()
        mine[i, halves] = (part[i, at(base, c, half)] + got1[i, halves]).astype(BF16)
        second = [remote(mine.at[i, at(base1, lax.rem(p + d, planes), quarter)],
                         got2.at[i, d - 1, quarters], there, d, plane_peers[d - 1])
                  for d in range(1, planes)]
        yield
        value = part[i, at(base, c * planes + p, quarter)] + got1[i, at(base1, p, quarter)]
        for d in range(1, planes):
            second[d - 1].wait()
            value = value + got2[i, d - 1, quarters].astype(F32)
        own[i, quarters] = value
        rest[i, quarters] = value.astype(BF16)
        third = [remote(rest.at[i, at(base2, lax.rem(z + d, depth), piece)],
                        got3.at[i, d - 1, pieces], there, planes - 1 + d, deep_peers[d - 1])
                 for d in range(1, depth)]
        yield
        value = own[i, at(base2, z, piece)]
        for d in range(1, depth):
            third[d - 1].wait()
            value = value + got3[i, d - 1, pieces].astype(F32)
        place = at(base, (c * planes + p) * depth + z, piece)
        total[i, place] = (value / scale).astype(BF16)
        for where, peers, first_sem in (
            (place, deep_peers, planes),
            (at(base, c * planes + p, quarter), plane_peers, 1),
            (at(base, c, half), [partner], 0),
        ):
            moved = [remote(total.at[i, where], total.at[i, where], back, first_sem + m, peer)
                     for m, peer in enumerate(peers)]
            yield
            for copy in moved:
                copy.wait()
        kept = pl.ds(base, min(size, wide - base))
        copy = pltpu.make_async_copy(total.at[i, kept], outs[i].at[kept], store.at[i, n])
        copy.start()
        yield copy

    return stages, [partner] + plane_peers + deep_peers


def on_device(features, grad_out, w1, w2, rulebook, live_blocks):
    offsets, chans = w1.shape[0], w1.shape[1]
    devices = lax.axis_size("region") * lax.axis_size("block")
    step = 16 * devices
    units = (offsets * chans + step - 1) // step
    parts = min(PARTS, units)
    cuts = [units * n // parts * step for n in range(parts + 1)]
    scale = float(features.shape[0] * devices) ** 0.5
    grad_in, *both = slab_step(
        features, grad_out, w1, w2, rulebook, live_blocks, cuts, scale)
    grad_w1, grad_w2 = (
        part.astype(F32).reshape(offsets, chans, chans) for part in both)
    return (grad_in, grad_w1, grad_w2)


def solution(mesh):
    return jax.shard_map(
        on_device,
        mesh=mesh,
        in_specs=(
            P(("region", "block"), None),
            P(("region", "block"), None),
            P(),
            P(),
            P(None, ("region", "block")),
            P(("region", "block")),
        ),
        out_specs=(P(("region", "block"), None), P(), P()),
        check_vma=False,
    )
```

```python
import functools

import jax
import jax.numpy as jnp
from jax import lax
from jax.experimental import pallas as pl
from jax.experimental.pallas import tpu as pltpu
from jax.sharding import PartitionSpec as P

BLOCK = 128
HALO = 128
NOWHERE = 4.0 * BLOCK
PARTS = 3
STEPS = 1
MESH = pl.DeviceIdType.MESH
F32 = jnp.float32
BF16 = jnp.bfloat16


def slab_kernel(
    region, length, scale, cuts,
    feat_in, gout_in, w1, w2, rule_in, live,
    grad_in, out1, out2,
    feat, gout, rule, w1v, w2v, w1c, w2c, w1t, ft, gt, ht, act, near, picks, spread, hidden,
    fin, gin, rin, hout, hin, load, send, recv, store,
    partial, total, held, sent, got1, got2, got3,
    send_there, recv_there, send_back, recv_back,
):
    rows, chans = feat_in.shape
    offsets = w1.shape[0]
    blocks = rows // BLOCK
    pairs = blocks // 2
    ext_blocks = blocks + 2
    wide = offsets * chans
    part_rows = partial.shape[1]
    me = lax.axis_index("block")
    left, right = me - 1, me + 1
    has_left, has_right = me > 0, me < length - 1

    loads = [pltpu.make_async_copy(src, dst, load.at[n]) for n, (src, dst) in enumerate((
        (feat_in, feat), (rule_in, rule), (gout_in, gout), (w1, w1v), (w2, w2v)))]
    for copy in loads:
        copy.start()

    def copies(i, low, high, arrived):
        down = pltpu.make_async_remote_copy(
            src_ref=low, dst_ref=arrived.at[1], send_sem=send.at[i, 0], recv_sem=recv.at[i, 0],
            device_id={"block": left}, device_id_type=MESH)
        up = pltpu.make_async_remote_copy(
            src_ref=high, dst_ref=arrived.at[0], send_sem=send.at[i, 1], recv_sem=recv.at[i, 1],
            device_id={"block": right}, device_id_type=MESH)
        return down, up

    def start(pair):
        down, up = pair
        pl.when(has_left)(down.start)
        pl.when(has_right)(up.start)

    def finish(pair):
        down, up = pair

        @pl.when(has_left)
        def _():
            down.wait_send()
            up.wait_recv()

        @pl.when(has_right)
        def _():
            up.wait_send()
            down.wait_recv()

    stages, peers = sum_stages(
        region, length, scale, cuts, wide, partial, total, (out1, out2), store, held, sent, got1, got2, got3,
        (send_there, recv_there), (send_back, recv_back))
    barrier = pltpu.get_barrier_semaphore()
    for peer in peers:
        pl.semaphore_signal(barrier, inc=1, device_id=peer, device_id_type=MESH)

    @pl.when(has_left)
    def _():
        pl.semaphore_signal(barrier, inc=1, device_id={"block": left}, device_id_type=MESH)

    @pl.when(has_right)
    def _():
        pl.semaphore_signal(barrier, inc=1, device_id={"block": right}, device_id_type=MESH)

    def entry(e):
        return slice(e * BLOCK, (e + 1) * BLOCK)

    def reach(rule_part, e):
        value = (rule_part - e * BLOCK).astype(F32)
        return jnp.where(rule_part == rows + 2 * HALO, NOWHERE, value)

    for copy in loads[:2]:
        copy.wait()
    for e in range(1, blocks + 1):
        ft[:, entry(e)] = feat[entry(e - 1)].T
        near[:, entry(e)] = reach(rule[:, entry(e - 1)], e)

    one, zero = jnp.ones((BLOCK, BLOCK), BF16), jnp.zeros((BLOCK, BLOCK), BF16)

    def steps(dim):
        base = lax.broadcasted_iota(jnp.int32, (BLOCK, BLOCK), dim)
        return [(base + d * BLOCK).astype(BF16) for d in (-1, 0, 1)]

    def row_of(k, begin):
        value = near[k:k + 1, pl.ds(pl.multiple_of(begin, BLOCK), BLOCK)].astype(BF16)
        return jnp.broadcast_to(value, (BLOCK, BLOCK))

    def gather(source, out, b, ks):
        at = steps(0)
        begin = pl.multiple_of(b * 2 * BLOCK, BLOCK)
        window = source[:, pl.ds(begin, 4 * BLOCK)]
        for k in ks:
            sides = [row_of(k, begin + (j + 1) * BLOCK) for j in range(2)]
            chosen = jnp.concatenate([
                jnp.concatenate([
                    jnp.where(sides[j] == at[i - j], one, zero) if 0 <= i - j < 3 else zero
                    for i in range(4)], 0)
                for j in range(2)], 1)
            out[entry(k), pl.ds(begin, 2 * BLOCK)] = jnp.dot(
                window, chosen, preferred_element_type=F32).astype(BF16)

    def scatter(source, out, b, ks):
        at = steps(1)
        begin = pl.multiple_of(b * 2 * BLOCK, BLOCK)
        window = source[:, pl.ds(begin, 4 * BLOCK)]
        for k in ks:
            sides = [row_of(k, begin + i * BLOCK).T for i in range(4)]
            chosen = jnp.concatenate([
                jnp.concatenate([
                    jnp.where(sides[i] == at[j - i + 2], one, zero) if 0 <= j - i + 2 < 3 else zero
                    for j in range(2)], 1)
                for i in range(4)], 0)
            out[entry(k), pl.ds(begin, 2 * BLOCK)] = jnp.dot(
                window, chosen, preferred_element_type=F32).astype(BF16)

    inner, outer = range(1, pairs - 1), (0, pairs - 1)
    every = range(offsets)

    def over(pair_blocks, job, source, out, ks):
        first, stride = pair_blocks[0], pair_blocks[-1] - pair_blocks[0]

        @pl.loop(0, len(pair_blocks))
        def _(n):
            job(source, out, first + n * stride // max(1, len(pair_blocks) - 1), ks)

    for e in (0, blocks + 1):
        ft[:, entry(e)] = jnp.zeros((chans, HALO), BF16)
    over(range(pairs - 1), gather, ft, picks, every)

    pl.semaphore_wait(
        barrier, len(peers) + has_left.astype(jnp.int32) + has_right.astype(jnp.int32))
    loads[2].wait()
    first, last = pl.ds(0, HALO), pl.ds(rows - HALO, HALO)
    halo_copies = [
        copies(0, feat.at[first], feat.at[last], fin),
        copies(1, rule.at[:, first], rule.at[:, last], rin),
        copies(2, gout.at[first], gout.at[last], gin),
    ]
    hidden_copies = copies(3, hout.at[0], hout.at[1], hin)
    for pair in halo_copies:
        start(pair)

    edge = jnp.zeros((HALO, chans), BF16)
    none = jnp.full((offsets, HALO), rows + 2 * HALO, jnp.int32)
    for side, missing in ((0, jnp.logical_not(has_left)), (1, jnp.logical_not(has_right))):
        @pl.when(missing)
        def _(side=side):
            fin[side] = edge
            gin[side] = edge
            hin[side] = edge
            rin[side] = none

    gather(ft, picks, pairs - 1, every)
    for e in range(1, blocks + 1):
        gt[:, entry(e)] = gout[entry(e - 1)].T
    for b in inner:
        scatter(gt, spread, b, every)
    for copy in loads[3:]:
        copy.wait()
    for k in range(offsets):
        w1c[:, entry(k)] = w1v[k]
        w1t[:, entry(k)] = w1v[k].T
        w2c[:, entry(k)] = w2v[k]

    for pair in halo_copies:
        finish(pair)
    for side, e, seen in ((0, 0, blocks), (1, blocks + 1, 1)):
        ft[:, entry(e)] = fin[side].T
        gt[:, entry(e)] = gin[side].T
        near[:, entry(e)] = reach(rin[side], seen)

    tail = part_rows - wide
    if tail:
        for i in range(2):
            partial[i, pl.ds(wide, tail)] = jnp.zeros((tail, chans), F32)

    count = len(cuts) - 1
    sums = [[stages(i, n) for n in range(count)] for i in range(2)]

    def poke(*which):
        for i, n in which:
            if 0 <= n < count:
                next(sums[i][n])

    spans = [range(min(offsets, lo // chans), min(offsets, hi // chans))
             for lo, hi in zip(cuts[:-1], cuts[1:])]

    def complete(e, u, step):
        at = steps(0)[step]
        cols = pl.ds((e - 1) * BLOCK, BLOCK)
        for k in range(0, offsets, 2):
            ks = range(k, min(k + 2, offsets))
            chosen = jnp.concatenate(
                [jnp.where(row_of(n, e * BLOCK) == at, one, zero) for n in ks], 1)
            got = jnp.dot(ft[:, entry(u)], chosen, preferred_element_type=F32).astype(BF16)
            for n in ks:
                picks[entry(n), cols] = picks[entry(n), cols] + got[:, entry(n - k)]

    complete(1, 0, 0)
    complete(blocks, blocks + 1, 2)
    value = jnp.dot(w1t[...], picks[...], preferred_element_type=F32)
    hidden[...] = value
    act[...] = (value / (1.0 + jnp.exp(-value))).astype(BF16)

    for n, ks in enumerate(spans):
        over(outer, scatter, gt, spread, ks)
        got = lax.dot_general(
            act[...], spread[pl.ds(ks[0] * chans, len(ks) * chans)], (((1,), (1,)), ((), ())),
            preferred_element_type=F32)
        for k in ks:
            partial[1, entry(k)] = got[:, entry(k - ks[0])]
        poke((1, n - 1), (1, n))

    grad_act = jnp.dot(w2c[...], spread[...], preferred_element_type=F32)
    value = hidden[...]
    sigma = 1.0 / (1.0 + jnp.exp(-value))
    slope = sigma * (1.0 + value * (1.0 - sigma))
    ht[:, pl.ds(HALO, rows)] = (grad_act * slope).astype(BF16)
    hout[0] = ht[:, entry(1)]
    hout[1] = ht[:, entry(blocks)]
    start(hidden_copies)
    poke((1, count - 1))

    turned = jnp.concatenate([ht[:, entry(e)].T for e in range(1, blocks + 1)], 0)
    for n, ks in enumerate(spans):
        at = pl.ds(ks[0] * chans, len(ks) * chans)
        partial[0, at] = jnp.dot(picks[at], turned, preferred_element_type=F32)
        poke((0, n), (0, n - 2))

    for b in inner:
        scatter(ht, spread, b, every)
    poke(*[(0, n) for n in range(max(0, count - 2), count)], (1, 0))
    finish(hidden_copies)
    ht[:, entry(0)] = hin[0]
    ht[:, entry(blocks + 1)] = hin[1]
    scatter(ht, spread, outer[0], every)
    poke((1, 1))
    scatter(ht, spread, outer[1], every)
    poke((1, 2))
    grad_feat = jnp.dot(w1c[...], spread[...], preferred_element_type=F32)
    for b in range(blocks):
        keep = live[b].astype(F32)
        grad_in[entry(b)] = (
            keep * (gout[entry(b)].astype(F32) + grad_feat[:, entry(b)].T)).astype(BF16)
    left_over = [sums[i][n] for n in range(count) for i in (1, 0)]
    stores = []
    while left_over:
        going = []
        for one_sum in left_over:
            copy = next(one_sum)
            if copy is None:
                going.append(one_sum)
            else:
                stores.append(copy)
        left_over = going
    for copy in stores:
        copy.wait()


def slab_step(features, grad_out, w1, w2, rulebook, live_blocks, cuts, scale):
    region, block = lax.axis_size("region"), lax.axis_size("block")
    planes, near, far = grouping(region, block)
    group = planes * near
    part_rows = cuts[-1]
    half = part_rows // 2
    piece = half // group
    count = group - 1 + far
    rows, chans = features.shape
    offsets = w1.shape[0]
    ext = rows + 2 * HALO
    wide = offsets * chans
    vmem = pl.BlockSpec(memory_space=pltpu.VMEM)
    hbm = pl.BlockSpec(memory_space=pl.ANY)
    return pl.pallas_call(
        functools.partial(slab_kernel, region, block, scale, cuts),
        out_shape=(
            jax.ShapeDtypeStruct((rows, chans), BF16),
            jax.ShapeDtypeStruct((wide, chans), BF16),
            jax.ShapeDtypeStruct((wide, chans), BF16),
        ),
        in_specs=[hbm, hbm, hbm, hbm, hbm, pl.BlockSpec(memory_space=pltpu.SMEM)],
        out_specs=(vmem, hbm, hbm),
        scratch_shapes=[
            pltpu.VMEM((rows, chans), BF16),
            pltpu.VMEM((rows, chans), BF16),
            pltpu.VMEM((offsets, rows), jnp.int32),
            pltpu.VMEM((offsets, chans, chans), BF16),
            pltpu.VMEM((offsets, chans, chans), BF16),
            pltpu.VMEM((chans, wide), BF16),
            pltpu.VMEM((chans, wide), BF16),
            pltpu.VMEM((chans, wide), BF16),
            pltpu.VMEM((chans, ext), BF16),
            pltpu.VMEM((chans, ext), BF16),
            pltpu.VMEM((chans, ext), BF16),
            pltpu.VMEM((chans, rows), BF16),
            pltpu.VMEM((offsets, ext), F32),
            pltpu.VMEM((wide, rows), BF16),
            pltpu.VMEM((wide, rows), BF16),
            pltpu.VMEM((chans, rows), F32),
            pltpu.VMEM((2, HALO, chans), BF16),
            pltpu.VMEM((2, HALO, chans), BF16),
            pltpu.VMEM((2, offsets, HALO), jnp.int32),
            pltpu.VMEM((2, chans, HALO), BF16),
            pltpu.VMEM((2, chans, HALO), BF16),
            pltpu.SemaphoreType.DMA((5,)),
            pltpu.SemaphoreType.DMA((4, 2)),
            pltpu.SemaphoreType.DMA((4, 2)),
            pltpu.SemaphoreType.DMA((2, len(cuts) - 1)),
            pltpu.VMEM((2, part_rows, chans), F32),
            pltpu.VMEM((2, part_rows, chans), BF16),
            pltpu.VMEM((2, piece, chans), BF16),
            pltpu.VMEM((2, half, chans), BF16),
            pltpu.VMEM((2, half, chans), F32),
            pltpu.VMEM((2, group - 1, piece, chans), BF16),
            pltpu.VMEM((2, far, piece, chans), BF16),
        ] + [pltpu.SemaphoreType.DMA((2, len(cuts) - 1, count))] * 4,
        compiler_params=pltpu.CompilerParams(
            collective_id=0, has_side_effects=True, vmem_limit_bytes=64000000),
    )(features, grad_out, w1, w2, rulebook, live_blocks)


def grouping(region, block):
    depth = block // 2
    near = 2 if depth % 2 == 0 else 1
    return region // 2 * 2, near, depth // near


def sum_stages(region, block, scale, cuts, wide, part, total, outs, store, held, sent, got1,
               got2, got3, there, back):
    planes, near, far = grouping(region, block)
    group = planes * near
    r, b = lax.axis_index("region"), lax.axis_index("block")
    c, y, x, z = lax.rem(r, 2), r // 2, lax.rem(b, 2), b // 2
    q = (y * 2 + x) * near + lax.rem(z, near)
    f = z // near

    def device(core, member, away):
        plane = member // near
        deep = away * near + lax.rem(member, near)
        return {"region": plane // 2 * 2 + core, "block": deep * 2 + lax.rem(plane, 2)}

    partner = device(1 - c, q, f)
    near_peers = [device(c, lax.rem(q + d, group), f) for d in range(1, group)]
    far_peers = [device(c, q, lax.rem(f + d, far)) for d in range(1, far)]

    def stages(i, n):
        base, size = cuts[n], cuts[n + 1] - cuts[n]
        half = size // 2
        piece = half // group
        base_half = base // 2
        base_piece = base_half // group

        def at(start, index, count):
            return pl.ds(pl.multiple_of(start + index * count, 16), count)

        def remote(src, dst, sems, m, peer):
            copy = pltpu.make_async_remote_copy(
                src_ref=src, dst_ref=dst, send_sem=sems[0].at[i, n, m],
                recv_sem=sems[1].at[i, n, m], device_id=peer, device_id_type=MESH)
            copy.start()
            return copy

        halves, pieces = pl.ds(base_half, half), pl.ds(base_piece, piece)

        first = remote(part.at[i, at(base, 1 - c, half)], got1.at[i, halves], there, 0, partner)
        yield
        first.wait()
        sent[i, halves] = (part[i, at(base, c, half)] + got1[i, halves]).astype(BF16)
        second = [remote(sent.at[i, at(base_half, lax.rem(q + d, group), piece)],
                         got2.at[i, d - 1, pieces], there, d, near_peers[d - 1])
                  for d in range(1, group)]
        yield
        value = part[i, at(base, c * group + q, piece)] + got1[i, at(base_half, q, piece)]
        for d in range(1, group):
            second[d - 1].wait()
            value = value + got2[i, d - 1, pieces].astype(F32)
        held[i, pieces] = value.astype(BF16)
        got3[i, 0, pieces] = held[i, pieces]
        third = [remote(held.at[i, pieces], got3.at[i, d, pieces], there, group - 1 + d,
                        far_peers[d - 1])
                 for d in range(1, far)]
        yield
        for copy in third:
            copy.wait()
        value = jnp.zeros((piece, part.shape[2]), F32)
        for d in range(far):
            value = value + got3[i, lax.rem(f + far - d, far), pieces].astype(F32)
        place = at(base, c * group + q, piece)
        total[i, place] = (value / scale).astype(BF16)
        for where, peers, sem in (
            (place, near_peers, 1),
            (at(base, c, half), [partner], 0),
        ):
            moved = [remote(total.at[i, where], total.at[i, where], back, sem + m, peer)
                     for m, peer in enumerate(peers)]
            yield
            for copy in moved:
                copy.wait()
        kept = pl.ds(base, min(size, wide - base))
        copy = pltpu.make_async_copy(total.at[i, kept], outs[i].at[kept], store.at[i, n])
        copy.start()
        yield copy

    return stages, [partner] + near_peers + far_peers


def widen_kernel(a, b, c, a_out, b_out, c_out):
    a_out[...] = a[...]
    b_out[...] = b[...].astype(F32)
    c_out[...] = c[...].astype(F32)


def widen(grad_in, part1, part2):
    rows, chans = grad_in.shape
    wide = part1.shape[0]
    steps = STEPS if rows % (16 * STEPS) == 0 and wide % (16 * STEPS) == 0 else 1

    def spec(count):
        return pl.BlockSpec((count // steps, chans), lambda n: (n, 0))

    return pl.pallas_call(
        widen_kernel,
        grid=(steps,),
        out_shape=(
            jax.ShapeDtypeStruct((rows, chans), BF16),
            jax.ShapeDtypeStruct((wide, chans), F32),
            jax.ShapeDtypeStruct((wide, chans), F32),
        ),
        in_specs=[spec(rows), spec(wide), spec(wide)],
        out_specs=(spec(rows), spec(wide), spec(wide)),
    )(grad_in, part1, part2)


def on_device(features, grad_out, w1, w2, rulebook, live_blocks):
    offsets, chans = w1.shape[0], w1.shape[1]
    region, block = lax.axis_size("region"), lax.axis_size("block")
    planes, near, far = grouping(region, block)
    step = 32 * planes * near
    units = (offsets * chans + step - 1) // step
    parts = min(PARTS, units)
    cuts = [units * n // parts * step for n in range(parts + 1)]
    scale = float(features.shape[0] * region * block) ** 0.5
    grad_in, *both = slab_step(
        features, grad_out, w1, w2, rulebook, live_blocks, cuts, scale)
    grad_in, grad_w1, grad_w2 = widen(grad_in, *both)
    return (grad_in, grad_w1.reshape(w1.shape), grad_w2.reshape(w2.shape))


def solution(mesh):
    return jax.shard_map(
        on_device,
        mesh=mesh,
        in_specs=(
            P(("region", "block"), None),
            P(("region", "block"), None),
            P(),
            P(),
            P(None, ("region", "block")),
            P(("region", "block")),
        ),
        out_specs=(P(("region", "block"), None), P(), P()),
        check_vma=False,
    )
```

```python
import functools

import jax
import jax.numpy as jnp
from jax import lax
from jax.experimental import pallas as pl
from jax.experimental.pallas import tpu as pltpu
from jax.sharding import PartitionSpec as P

BLOCK = 128
HALO = 128
NOWHERE = 4.0 * BLOCK
SHARES = (0, 6, 11, 14)
STEPS = 4
MESH = pl.DeviceIdType.MESH
F32 = jnp.float32
BF16 = jnp.bfloat16


def slab_kernel(
    region, length, scale, cuts,
    feat_in, gout_in, w1, w2, rule_in, live,
    grad_in_out, out1, out2,
    grad_in, feat, gout, rule, w1v, w2v, w1c, w2c, w1t, ft, gt, ht, act, near, picks, spread, hidden,
    fin, gin, rin, hout, hin, load, send, recv, store,
    partial, total, held, sent, got1, got2, got3,
    send_there, recv_there, send_back, recv_back,
):
    rows, chans = feat_in.shape
    offsets = w1.shape[0]
    blocks = rows // BLOCK
    pairs = blocks // 2
    ext_blocks = blocks + 2
    wide = offsets * chans
    part_rows = partial.shape[1]
    me = lax.axis_index("block")
    left, right = me - 1, me + 1
    has_left, has_right = me > 0, me < length - 1

    loads = [pltpu.make_async_copy(src, dst, load.at[n]) for n, (src, dst) in enumerate((
        (feat_in, feat), (rule_in, rule), (gout_in, gout), (w1, w1v), (w2, w2v)))]
    for copy in loads:
        copy.start()

    def copies(i, low, high, arrived):
        down = pltpu.make_async_remote_copy(
            src_ref=low, dst_ref=arrived.at[1], send_sem=send.at[i, 0], recv_sem=recv.at[i, 0],
            device_id={"block": left}, device_id_type=MESH)
        up = pltpu.make_async_remote_copy(
            src_ref=high, dst_ref=arrived.at[0], send_sem=send.at[i, 1], recv_sem=recv.at[i, 1],
            device_id={"block": right}, device_id_type=MESH)
        return down, up

    def start(pair):
        down, up = pair
        pl.when(has_left)(down.start)
        pl.when(has_right)(up.start)

    def finish(pair):
        down, up = pair

        @pl.when(has_left)
        def _():
            down.wait_send()
            up.wait_recv()

        @pl.when(has_right)
        def _():
            up.wait_send()
            down.wait_recv()

    stages, peers = sum_stages(
        region, length, scale, cuts, wide, partial, total, (out1, out2), store, held, sent, got1, got2, got3,
        (send_there, recv_there), (send_back, recv_back))
    barrier = pltpu.get_barrier_semaphore()
    for peer in peers:
        pl.semaphore_signal(barrier, inc=1, device_id=peer, device_id_type=MESH)

    @pl.when(has_left)
    def _():
        pl.semaphore_signal(barrier, inc=1, device_id={"block": left}, device_id_type=MESH)

    @pl.when(has_right)
    def _():
        pl.semaphore_signal(barrier, inc=1, device_id={"block": right}, device_id_type=MESH)

    def entry(e):
        return slice(e * BLOCK, (e + 1) * BLOCK)

    def reach(rule_part, e):
        value = (rule_part - e * BLOCK).astype(F32)
        return jnp.where(rule_part == rows + 2 * HALO, NOWHERE, value)

    for copy in loads[:2]:
        copy.wait()
    for e in range(1, blocks + 1):
        ft[:, entry(e)] = feat[entry(e - 1)].T
        near[:, entry(e)] = reach(rule[:, entry(e - 1)], e)

    one, zero = jnp.ones((BLOCK, BLOCK), BF16), jnp.zeros((BLOCK, BLOCK), BF16)

    def steps(dim):
        base = lax.broadcasted_iota(jnp.int32, (BLOCK, BLOCK), dim)
        return [(base + d * BLOCK).astype(BF16) for d in (-1, 0, 1)]

    def row_of(k, begin):
        value = near[k:k + 1, pl.ds(pl.multiple_of(begin, BLOCK), BLOCK)].astype(BF16)
        return jnp.broadcast_to(value, (BLOCK, BLOCK))

    def gather(source, out, b, ks):
        at = steps(0)
        begin = pl.multiple_of(b * 2 * BLOCK, BLOCK)
        window = source[:, pl.ds(begin, 4 * BLOCK)]
        for k in ks:
            sides = [row_of(k, begin + (j + 1) * BLOCK) for j in range(2)]
            chosen = jnp.concatenate([
                jnp.concatenate([
                    jnp.where(sides[j] == at[i - j], one, zero) if 0 <= i - j < 3 else zero
                    for i in range(4)], 0)
                for j in range(2)], 1)
            out[entry(k), pl.ds(begin, 2 * BLOCK)] = jnp.dot(
                window, chosen, preferred_element_type=F32).astype(BF16)

    def scatter(source, out, b, ks):
        at = steps(1)
        begin = pl.multiple_of(b * 2 * BLOCK, BLOCK)
        window = source[:, pl.ds(begin, 4 * BLOCK)]
        for k in ks:
            sides = [row_of(k, begin + i * BLOCK).T for i in range(4)]
            chosen = jnp.concatenate([
                jnp.concatenate([
                    jnp.where(sides[i] == at[j - i + 2], one, zero) if 0 <= j - i + 2 < 3 else zero
                    for j in range(2)], 1)
                for i in range(4)], 0)
            out[entry(k), pl.ds(begin, 2 * BLOCK)] = jnp.dot(
                window, chosen, preferred_element_type=F32).astype(BF16)

    inner, outer = range(1, pairs - 1), (0, pairs - 1)
    every = range(offsets)

    def over(pair_blocks, job, source, out, ks):
        first, stride = pair_blocks[0], pair_blocks[-1] - pair_blocks[0]

        @pl.loop(0, len(pair_blocks))
        def _(n):
            job(source, out, first + n * stride // max(1, len(pair_blocks) - 1), ks)

    for e in (0, blocks + 1):
        ft[:, entry(e)] = jnp.zeros((chans, HALO), BF16)
    over(range(pairs - 1), gather, ft, picks, every)

    pl.semaphore_wait(
        barrier, len(peers) + has_left.astype(jnp.int32) + has_right.astype(jnp.int32))
    loads[2].wait()
    first, last = pl.ds(0, HALO), pl.ds(rows - HALO, HALO)
    halo_copies = [
        copies(0, feat.at[first], feat.at[last], fin),
        copies(1, rule.at[:, first], rule.at[:, last], rin),
        copies(2, gout.at[first], gout.at[last], gin),
    ]
    hidden_copies = copies(3, hout.at[0], hout.at[1], hin)
    for pair in halo_copies:
        start(pair)

    edge = jnp.zeros((HALO, chans), BF16)
    none = jnp.full((offsets, HALO), rows + 2 * HALO, jnp.int32)
    for side, missing in ((0, jnp.logical_not(has_left)), (1, jnp.logical_not(has_right))):
        @pl.when(missing)
        def _(side=side):
            fin[side] = edge
            gin[side] = edge
            hin[side] = edge
            rin[side] = none

    gather(ft, picks, pairs - 1, every)
    for e in range(1, blocks + 1):
        gt[:, entry(e)] = gout[entry(e - 1)].T
    for b in inner:
        scatter(gt, spread, b, every)
    for copy in loads[3:]:
        copy.wait()
    for k in range(offsets):
        w1c[:, entry(k)] = w1v[k]
        w1t[:, entry(k)] = w1v[k].T
        w2c[:, entry(k)] = w2v[k]

    for pair in halo_copies:
        finish(pair)
    for side, e, seen in ((0, 0, blocks), (1, blocks + 1, 1)):
        ft[:, entry(e)] = fin[side].T
        gt[:, entry(e)] = gin[side].T
        near[:, entry(e)] = reach(rin[side], seen)

    tail = part_rows - wide
    if tail:
        for i in range(2):
            partial[i, pl.ds(wide, tail)] = jnp.zeros((tail, chans), F32)

    count = len(cuts) - 1
    sums = [[stages(i, n) for n in range(count)] for i in range(2)]

    def poke(*which):
        for i, n in which:
            if 0 <= n < count:
                next(sums[i][n])

    spans = [range(min(offsets, lo // chans), min(offsets, hi // chans))
             for lo, hi in zip(cuts[:-1], cuts[1:])]

    def complete(e, u, step):
        at = steps(0)[step]
        cols = pl.ds((e - 1) * BLOCK, BLOCK)
        for k in range(0, offsets, 2):
            ks = range(k, min(k + 2, offsets))
            chosen = jnp.concatenate(
                [jnp.where(row_of(n, e * BLOCK) == at, one, zero) for n in ks], 1)
            got = jnp.dot(ft[:, entry(u)], chosen, preferred_element_type=F32).astype(BF16)
            for n in ks:
                picks[entry(n), cols] = picks[entry(n), cols] + got[:, entry(n - k)]

    complete(1, 0, 0)
    complete(blocks, blocks + 1, 2)
    value = jnp.dot(w1t[...], picks[...], preferred_element_type=F32)
    hidden[...] = value
    act[...] = (value / (1.0 + jnp.exp(-value))).astype(BF16)

    for n, ks in enumerate(spans):
        over(outer, scatter, gt, spread, ks)
        got = lax.dot_general(
            act[...], spread[pl.ds(ks[0] * chans, len(ks) * chans)], (((1,), (1,)), ((), ())),
            preferred_element_type=F32)
        for k in ks:
            partial[1, entry(k)] = got[:, entry(k - ks[0])]
        poke((1, n - 1), (1, n))

    grad_act = jnp.dot(w2c[...], spread[...], preferred_element_type=F32)
    value = hidden[...]
    sigma = 1.0 / (1.0 + jnp.exp(-value))
    slope = sigma * (1.0 + value * (1.0 - sigma))
    ht[:, pl.ds(HALO, rows)] = (grad_act * slope).astype(BF16)
    hout[0] = ht[:, entry(1)]
    hout[1] = ht[:, entry(blocks)]
    start(hidden_copies)
    poke((1, count - 1))

    turned = jnp.concatenate([ht[:, entry(e)].T for e in range(1, blocks + 1)], 0)
    for n, ks in enumerate(spans):
        at = pl.ds(ks[0] * chans, len(ks) * chans)
        partial[0, at] = jnp.dot(picks[at], turned, preferred_element_type=F32)
        poke((0, n), (0, n - 2))

    for b in inner:
        scatter(ht, spread, b, every)
    poke(*[(0, n) for n in range(max(0, count - 2), count)], (1, 0))
    finish(hidden_copies)
    ht[:, entry(0)] = hin[0]
    ht[:, entry(blocks + 1)] = hin[1]
    scatter(ht, spread, outer[0], every)
    poke((1, 1))
    scatter(ht, spread, outer[1], every)
    poke((1, 2))
    grad_feat = jnp.dot(w1c[...], spread[...], preferred_element_type=F32)
    for b in range(blocks):
        keep = live[b].astype(F32)
        grad_in[entry(b)] = (
            keep * (gout[entry(b)].astype(F32) + grad_feat[:, entry(b)].T)).astype(BF16)
    left_over = [sums[i][n] for n in range(count) for i in (1, 0)]
    stores = [pltpu.make_async_copy(grad_in, grad_in_out, load.at[5])]
    stores[0].start()
    while left_over:
        going = []
        for one_sum in left_over:
            copy = next(one_sum)
            if copy is None:
                going.append(one_sum)
            else:
                stores.append(copy)
        left_over = going
    for copy in stores:
        copy.wait()


def slab_step(features, grad_out, w1, w2, rulebook, live_blocks, cuts, scale):
    region, block = lax.axis_size("region"), lax.axis_size("block")
    planes, near, far = grouping(region, block)
    group = planes * near
    part_rows = cuts[-1]
    half = part_rows // 2
    piece = half // group
    count = group - 1 + far
    rows, chans = features.shape
    offsets = w1.shape[0]
    ext = rows + 2 * HALO
    wide = offsets * chans
    vmem = pl.BlockSpec(memory_space=pltpu.VMEM)
    hbm = pl.BlockSpec(memory_space=pl.ANY)
    return pl.pallas_call(
        functools.partial(slab_kernel, region, block, scale, cuts),
        out_shape=(
            jax.ShapeDtypeStruct((rows, chans), BF16),
            jax.ShapeDtypeStruct((wide, chans), BF16),
            jax.ShapeDtypeStruct((wide, chans), BF16),
        ),
        in_specs=[hbm, hbm, hbm, hbm, hbm, pl.BlockSpec(memory_space=pltpu.SMEM)],
        out_specs=(hbm, hbm, hbm),
        scratch_shapes=[
            pltpu.VMEM((rows, chans), BF16),
            pltpu.VMEM((rows, chans), BF16),
            pltpu.VMEM((rows, chans), BF16),
            pltpu.VMEM((offsets, rows), jnp.int32),
            pltpu.VMEM((offsets, chans, chans), BF16),
            pltpu.VMEM((offsets, chans, chans), BF16),
            pltpu.VMEM((chans, wide), BF16),
            pltpu.VMEM((chans, wide), BF16),
            pltpu.VMEM((chans, wide), BF16),
            pltpu.VMEM((chans, ext), BF16),
            pltpu.VMEM((chans, ext), BF16),
            pltpu.VMEM((chans, ext), BF16),
            pltpu.VMEM((chans, rows), BF16),
            pltpu.VMEM((offsets, ext), F32),
            pltpu.VMEM((wide, rows), BF16),
            pltpu.VMEM((wide, rows), BF16),
            pltpu.VMEM((chans, rows), F32),
            pltpu.VMEM((2, HALO, chans), BF16),
            pltpu.VMEM((2, HALO, chans), BF16),
            pltpu.VMEM((2, offsets, HALO), jnp.int32),
            pltpu.VMEM((2, chans, HALO), BF16),
            pltpu.VMEM((2, chans, HALO), BF16),
            pltpu.SemaphoreType.DMA((6,)),
            pltpu.SemaphoreType.DMA((4, 2)),
            pltpu.SemaphoreType.DMA((4, 2)),
            pltpu.SemaphoreType.DMA((2, len(cuts) - 1)),
            pltpu.VMEM((2, part_rows, chans), F32),
            pltpu.VMEM((2, part_rows, chans), BF16),
            pltpu.VMEM((2, piece, chans), BF16),
            pltpu.VMEM((2, half, chans), BF16),
            pltpu.VMEM((2, half, chans), F32),
            pltpu.VMEM((2, group - 1, piece, chans), BF16),
            pltpu.VMEM((2, far, piece, chans), BF16),
        ] + [pltpu.SemaphoreType.DMA((2, len(cuts) - 1, count))] * 4,
        compiler_params=pltpu.CompilerParams(
            collective_id=0, has_side_effects=True, vmem_limit_bytes=64000000),
    )(features, grad_out, w1, w2, rulebook, live_blocks)


def grouping(region, block):
    depth = block // 2
    near = 2 if depth % 2 == 0 else 1
    return region // 2 * 2, near, depth // near


def sum_stages(region, block, scale, cuts, wide, part, total, outs, store, held, sent, got1,
               got2, got3, there, back):
    planes, near, far = grouping(region, block)
    group = planes * near
    r, b = lax.axis_index("region"), lax.axis_index("block")
    c, y, x, z = lax.rem(r, 2), r // 2, lax.rem(b, 2), b // 2
    q = (y * 2 + x) * near + lax.rem(z, near)
    f = z // near

    def device(core, member, away):
        plane = member // near
        deep = away * near + lax.rem(member, near)
        return {"region": plane // 2 * 2 + core, "block": deep * 2 + lax.rem(plane, 2)}

    partner = device(1 - c, q, f)
    near_peers = [device(c, lax.rem(q + d, group), f) for d in range(1, group)]
    far_peers = [device(c, q, lax.rem(f + d, far)) for d in range(1, far)]

    def stages(i, n):
        base, size = cuts[n], cuts[n + 1] - cuts[n]
        half = size // 2
        piece = half // group
        base_half = base // 2
        base_piece = base_half // group

        def at(start, index, count):
            return pl.ds(pl.multiple_of(start + index * count, 16), count)

        def remote(src, dst, sems, m, peer):
            copy = pltpu.make_async_remote_copy(
                src_ref=src, dst_ref=dst, send_sem=sems[0].at[i, n, m],
                recv_sem=sems[1].at[i, n, m], device_id=peer, device_id_type=MESH)
            copy.start()
            return copy

        halves, pieces = pl.ds(base_half, half), pl.ds(base_piece, piece)

        first = remote(part.at[i, at(base, 1 - c, half)], got1.at[i, halves], there, 0, partner)
        yield
        first.wait()
        sent[i, halves] = (part[i, at(base, c, half)] + got1[i, halves]).astype(BF16)
        second = [remote(sent.at[i, at(base_half, lax.rem(q + d, group), piece)],
                         got2.at[i, d - 1, pieces], there, d, near_peers[d - 1])
                  for d in range(1, group)]
        yield
        value = part[i, at(base, c * group + q, piece)] + got1[i, at(base_half, q, piece)]
        for d in range(1, group):
            second[d - 1].wait()
            value = value + got2[i, d - 1, pieces].astype(F32)
        held[i, pieces] = value.astype(BF16)
        got3[i, 0, pieces] = held[i, pieces]
        third = [remote(held.at[i, pieces], got3.at[i, d, pieces], there, group - 1 + d,
                        far_peers[d - 1])
                 for d in range(1, far)]
        yield
        for copy in third:
            copy.wait()
        value = jnp.zeros((piece, part.shape[2]), F32)
        for d in range(far):
            value = value + got3[i, lax.rem(f + far - d, far), pieces].astype(F32)
        place = at(base, c * group + q, piece)
        total[i, place] = (value / scale).astype(BF16)
        for where, peers, sem in (
            (place, near_peers, 1),
            (at(base, c, half), [partner], 0),
        ):
            moved = [remote(total.at[i, where], total.at[i, where], back, sem + m, peer)
                     for m, peer in enumerate(peers)]
            yield
            for copy in moved:
                copy.wait()
        kept = pl.ds(base, min(size, wide - base))
        copy = pltpu.make_async_copy(total.at[i, kept], outs[i].at[kept], store.at[i, n])
        copy.start()
        yield copy

    return stages, [partner] + near_peers + far_peers


def widen_kernel(a, b, c, a_out, b_out, c_out, kept, narrow, wide, loaded, stored, through):
    count = loaded.shape[1]
    rows = b.shape[0] // count
    inward = pltpu.make_async_copy(a, kept, through.at[0])
    outward = pltpu.make_async_copy(kept, a_out, through.at[1])
    pieces = [(i, n, pl.ds(n * rows, rows)) for i in range(2) for n in range(count)]
    loads = [pltpu.make_async_copy((b, c)[i].at[at], narrow.at[i, at], loaded.at[i, n])
             for i, n, at in pieces]
    stores = [pltpu.make_async_copy(wide.at[i, at], (b_out, c_out)[i].at[at], stored.at[i, n])
              for i, n, at in pieces]
    for copy in loads:
        copy.start()
    inward.start()
    for (i, n, at), load, store in zip(pieces, loads, stores):
        load.wait()
        wide[i, at] = narrow[i, at].astype(F32)
        store.start()
    inward.wait()
    outward.start()
    for copy in stores:
        copy.wait()
    outward.wait()


def widen(grad_in, part1, part2):
    rows, chans = grad_in.shape
    wide = part1.shape[0]
    steps = STEPS if wide % (16 * STEPS) == 0 else 1
    hbm = pl.BlockSpec(memory_space=pl.ANY)
    return pl.pallas_call(
        widen_kernel,
        out_shape=(
            jax.ShapeDtypeStruct((rows, chans), BF16),
            jax.ShapeDtypeStruct((wide, chans), F32),
            jax.ShapeDtypeStruct((wide, chans), F32),
        ),
        in_specs=[hbm] * 3,
        out_specs=(hbm,) * 3,
        scratch_shapes=[
            pltpu.VMEM((rows, chans), BF16),
            pltpu.VMEM((2, wide, chans), BF16),
            pltpu.VMEM((2, wide, chans), F32),
            pltpu.SemaphoreType.DMA((2, steps)),
            pltpu.SemaphoreType.DMA((2, steps)),
            pltpu.SemaphoreType.DMA((2,)),
        ],
        compiler_params=pltpu.CompilerParams(vmem_limit_bytes=64000000),
    )(grad_in, part1, part2)


def on_device(features, grad_out, w1, w2, rulebook, live_blocks):
    offsets, chans = w1.shape[0], w1.shape[1]
    region, block = lax.axis_size("region"), lax.axis_size("block")
    planes, near, far = grouping(region, block)
    step = 32 * planes * near
    units = (offsets * chans + step - 1) // step
    cuts = sorted({units * share // SHARES[-1] * step for share in SHARES})
    scale = float(features.shape[0] * region * block) ** 0.5
    grad_in, *both = slab_step(
        features, grad_out, w1, w2, rulebook, live_blocks, cuts, scale)
    grad_in, grad_w1, grad_w2 = widen(grad_in, *both)
    return (grad_in, grad_w1.reshape(w1.shape), grad_w2.reshape(w2.shape))


def solution(mesh):
    return jax.shard_map(
        on_device,
        mesh=mesh,
        in_specs=(
            P(("region", "block"), None),
            P(("region", "block"), None),
            P(),
            P(),
            P(None, ("region", "block")),
            P(("region", "block")),
        ),
        out_specs=(P(("region", "block"), None), P(), P()),
        check_vma=False,
    )
```

```python
import functools

import jax
import jax.numpy as jnp
from jax import lax
from jax.experimental import pallas as pl
from jax.experimental.pallas import tpu as pltpu
from jax.sharding import PartitionSpec as P

BLOCK = 128
HALO = 128
NOWHERE = 4.0 * BLOCK
SHARES = (0, 6, 11, 14)
STEPS = 4
MESH = pl.DeviceIdType.MESH
F32 = jnp.float32
BF16 = jnp.bfloat16


def slab_kernel(
    region, length, scale, cuts,
    feat_in, gout_in, w1, w2, rule_in, live,
    grad_in_out, out1, out2,
    grad_in, feat, gout, rule, w1v, w2v, w1c, w2c, w1t, ft, gt, ht, act, near, picks, spread, hidden,
    fin, gin, rin, hout, hin, load, send, recv, store,
    partial, total, held, sent, got1, got2, got3,
    send_there, recv_there, send_back, recv_back,
):
    rows, chans = feat_in.shape
    offsets = w1.shape[0]
    blocks = rows // BLOCK
    pairs = blocks // 2
    ext_blocks = blocks + 2
    wide = offsets * chans
    part_rows = partial.shape[1]
    me = lax.axis_index("block")
    left, right = me - 1, me + 1
    has_left, has_right = me > 0, me < length - 1

    loads = [pltpu.make_async_copy(src, dst, load.at[n]) for n, (src, dst) in enumerate((
        (feat_in, feat), (rule_in, rule), (gout_in, gout), (w1, w1v), (w2, w2v)))]
    for copy in loads:
        copy.start()

    def copies(i, low, high, arrived):
        down = pltpu.make_async_remote_copy(
            src_ref=low, dst_ref=arrived.at[1], send_sem=send.at[i, 0], recv_sem=recv.at[i, 0],
            device_id={"block": left}, device_id_type=MESH)
        up = pltpu.make_async_remote_copy(
            src_ref=high, dst_ref=arrived.at[0], send_sem=send.at[i, 1], recv_sem=recv.at[i, 1],
            device_id={"block": right}, device_id_type=MESH)
        return down, up

    def start(pair):
        down, up = pair
        pl.when(has_left)(down.start)
        pl.when(has_right)(up.start)

    def finish(pair):
        down, up = pair

        @pl.when(has_left)
        def _():
            down.wait_send()
            up.wait_recv()

        @pl.when(has_right)
        def _():
            up.wait_send()
            down.wait_recv()

    stages, peers = sum_stages(
        region, length, scale, cuts, wide, partial, total, (out1, out2), store, held, sent, got1, got2, got3,
        (send_there, recv_there), (send_back, recv_back))
    barrier = pltpu.get_barrier_semaphore()
    for peer in peers:
        pl.semaphore_signal(barrier, inc=1, device_id=peer, device_id_type=MESH)

    @pl.when(has_left)
    def _():
        pl.semaphore_signal(barrier, inc=1, device_id={"block": left}, device_id_type=MESH)

    @pl.when(has_right)
    def _():
        pl.semaphore_signal(barrier, inc=1, device_id={"block": right}, device_id_type=MESH)

    def entry(e):
        return slice(e * BLOCK, (e + 1) * BLOCK)

    def reach(rule_part, e):
        value = (rule_part - e * BLOCK).astype(F32)
        return jnp.where(rule_part == rows + 2 * HALO, NOWHERE, value)

    for copy in loads[:2]:
        copy.wait()
    for e in range(1, blocks + 1):
        ft[:, entry(e)] = feat[entry(e - 1)].T
        near[:, entry(e)] = reach(rule[:, entry(e - 1)], e)

    one, zero = jnp.ones((BLOCK, BLOCK), BF16), jnp.zeros((BLOCK, BLOCK), BF16)

    def steps(dim):
        base = lax.broadcasted_iota(jnp.int32, (BLOCK, BLOCK), dim)
        return [(base + d * BLOCK).astype(BF16) for d in (-1, 0, 1)]

    def row_of(k, begin):
        value = near[k:k + 1, pl.ds(pl.multiple_of(begin, BLOCK), BLOCK)].astype(BF16)
        return jnp.broadcast_to(value, (BLOCK, BLOCK))

    def gather(source, out, b, ks):
        at = steps(0)
        begin = pl.multiple_of(b * 2 * BLOCK, BLOCK)
        window = source[:, pl.ds(begin, 4 * BLOCK)]
        for k in ks:
            sides = [row_of(k, begin + (j + 1) * BLOCK) for j in range(2)]
            chosen = jnp.concatenate([
                jnp.concatenate([
                    jnp.where(sides[j] == at[i - j], one, zero) if 0 <= i - j < 3 else zero
                    for i in range(4)], 0)
                for j in range(2)], 1)
            out[entry(k), pl.ds(begin, 2 * BLOCK)] = jnp.dot(
                window, chosen, preferred_element_type=F32).astype(BF16)

    def scatter(source, out, b, ks):
        at = steps(1)
        begin = pl.multiple_of(b * 2 * BLOCK, BLOCK)
        window = source[:, pl.ds(begin, 4 * BLOCK)]
        for k in ks:
            sides = [row_of(k, begin + i * BLOCK).T for i in range(4)]
            chosen = jnp.concatenate([
                jnp.concatenate([
                    jnp.where(sides[i] == at[j - i + 2], one, zero) if 0 <= j - i + 2 < 3 else zero
                    for j in range(2)], 1)
                for i in range(4)], 0)
            out[entry(k), pl.ds(begin, 2 * BLOCK)] = jnp.dot(
                window, chosen, preferred_element_type=F32).astype(BF16)

    inner, outer = range(1, pairs - 1), (0, pairs - 1)
    every = range(offsets)

    def over(pair_blocks, job, source, out, ks):
        first, stride = pair_blocks[0], pair_blocks[-1] - pair_blocks[0]

        @pl.loop(0, len(pair_blocks))
        def _(n):
            job(source, out, first + n * stride // max(1, len(pair_blocks) - 1), ks)

    for e in (0, blocks + 1):
        ft[:, entry(e)] = jnp.zeros((chans, HALO), BF16)
    over(range(pairs - 1), gather, ft, picks, every)

    pl.semaphore_wait(
        barrier, len(peers) + has_left.astype(jnp.int32) + has_right.astype(jnp.int32))
    loads[2].wait()
    first, last = pl.ds(0, HALO), pl.ds(rows - HALO, HALO)
    halo_copies = [
        copies(0, feat.at[first], feat.at[last], fin),
        copies(1, rule.at[:, first], rule.at[:, last], rin),
        copies(2, gout.at[first], gout.at[last], gin),
    ]
    hidden_copies = copies(3, hout.at[0], hout.at[1], hin)
    for pair in halo_copies:
        start(pair)

    edge = jnp.zeros((HALO, chans), BF16)
    none = jnp.full((offsets, HALO), rows + 2 * HALO, jnp.int32)
    for side, missing in ((0, jnp.logical_not(has_left)), (1, jnp.logical_not(has_right))):
        @pl.when(missing)
        def _(side=side):
            fin[side] = edge
            gin[side] = edge
            hin[side] = edge
            rin[side] = none

    gather(ft, picks, pairs - 1, every)
    for e in range(1, blocks + 1):
        gt[:, entry(e)] = gout[entry(e - 1)].T
    for b in inner:
        scatter(gt, spread, b, every)
    for copy in loads[3:]:
        copy.wait()
    for k in range(offsets):
        w1c[:, entry(k)] = w1v[k]
        w1t[:, entry(k)] = w1v[k].T
        w2c[:, entry(k)] = w2v[k]

    for pair in halo_copies:
        finish(pair)
    for side, e, seen in ((0, 0, blocks), (1, blocks + 1, 1)):
        ft[:, entry(e)] = fin[side].T
        gt[:, entry(e)] = gin[side].T
        near[:, entry(e)] = reach(rin[side], seen)

    tail = part_rows - wide
    if tail:
        for i in range(2):
            partial[i, pl.ds(wide, tail)] = jnp.zeros((tail, chans), F32)

    count = len(cuts) - 1
    sums = [[stages(i, n) for n in range(count)] for i in range(2)]

    def poke(*which):
        for i, n in which:
            if 0 <= n < count:
                next(sums[i][n])

    spans = [range(min(offsets, lo // chans), min(offsets, hi // chans))
             for lo, hi in zip(cuts[:-1], cuts[1:])]

    def complete(e, u, step):
        at = steps(0)[step]
        cols = pl.ds((e - 1) * BLOCK, BLOCK)
        for k in range(0, offsets, 2):
            ks = range(k, min(k + 2, offsets))
            chosen = jnp.concatenate(
                [jnp.where(row_of(n, e * BLOCK) == at, one, zero) for n in ks], 1)
            got = jnp.dot(ft[:, entry(u)], chosen, preferred_element_type=F32).astype(BF16)
            for n in ks:
                picks[entry(n), cols] = picks[entry(n), cols] + got[:, entry(n - k)]

    complete(1, 0, 0)
    complete(blocks, blocks + 1, 2)
    value = jnp.dot(w1t[...], picks[...], preferred_element_type=F32)
    hidden[...] = value
    act[...] = (value / (1.0 + jnp.exp(-value))).astype(BF16)

    for n, ks in enumerate(spans):
        over(outer, scatter, gt, spread, ks)
        got = lax.dot_general(
            act[...], spread[pl.ds(ks[0] * chans, len(ks) * chans)], (((1,), (1,)), ((), ())),
            preferred_element_type=F32)
        for k in ks:
            partial[1, entry(k)] = got[:, entry(k - ks[0])]
        poke((1, n - 1), (1, n))

    grad_act = jnp.dot(w2c[...], spread[...], preferred_element_type=F32)
    value = hidden[...]
    sigma = 1.0 / (1.0 + jnp.exp(-value))
    slope = sigma * (1.0 + value * (1.0 - sigma))
    ht[:, pl.ds(HALO, rows)] = (grad_act * slope).astype(BF16)
    hout[0] = ht[:, entry(1)]
    hout[1] = ht[:, entry(blocks)]
    start(hidden_copies)
    poke((1, count - 1))

    turned = jnp.concatenate([ht[:, entry(e)].T for e in range(1, blocks + 1)], 0)
    for n, ks in enumerate(spans):
        at = pl.ds(ks[0] * chans, len(ks) * chans)
        partial[0, at] = jnp.dot(picks[at], turned, preferred_element_type=F32)
        poke((0, n), (0, n - 2))

    for b in inner:
        scatter(ht, spread, b, every)
    poke(*[(0, n) for n in range(max(0, count - 2), count)], (1, 0))
    finish(hidden_copies)
    ht[:, entry(0)] = hin[0]
    ht[:, entry(blocks + 1)] = hin[1]
    scatter(ht, spread, outer[0], every)
    poke((1, 1))
    scatter(ht, spread, outer[1], every)
    poke((1, 2))
    grad_feat = jnp.dot(w1c[...], spread[...], preferred_element_type=F32)
    for b in range(blocks):
        keep = live[b].astype(F32)
        grad_in[entry(b)] = (
            keep * (gout[entry(b)].astype(F32) + grad_feat[:, entry(b)].T)).astype(BF16)
    left_over = [sums[i][n] for n in range(count) for i in (1, 0)]
    stores = [pltpu.make_async_copy(grad_in, grad_in_out, load.at[5])]
    stores[0].start()
    while left_over:
        going = []
        for one_sum in left_over:
            copy = next(one_sum)
            if copy is None:
                going.append(one_sum)
            else:
                stores.append(copy)
        left_over = going
    for copy in stores:
        copy.wait()


def slab_step(features, grad_out, w1, w2, rulebook, live_blocks, cuts, scale):
    region, block = lax.axis_size("region"), lax.axis_size("block")
    planes, near, far = grouping(region, block)
    group = planes * near
    part_rows = cuts[-1]
    half = part_rows // 2
    piece = half // group
    count = group - 1 + far
    rows, chans = features.shape
    offsets = w1.shape[0]
    ext = rows + 2 * HALO
    wide = offsets * chans
    vmem = pl.BlockSpec(memory_space=pltpu.VMEM)
    hbm = pl.BlockSpec(memory_space=pl.ANY)
    return pl.pallas_call(
        functools.partial(slab_kernel, region, block, scale, cuts),
        out_shape=(
            jax.ShapeDtypeStruct((rows, chans), BF16),
            jax.ShapeDtypeStruct((wide, chans), BF16),
            jax.ShapeDtypeStruct((wide, chans), BF16),
        ),
        in_specs=[hbm, hbm, hbm, hbm, hbm, pl.BlockSpec(memory_space=pltpu.SMEM)],
        out_specs=(hbm, hbm, hbm),
        scratch_shapes=[
            pltpu.VMEM((rows, chans), BF16),
            pltpu.VMEM((rows, chans), BF16),
            pltpu.VMEM((rows, chans), BF16),
            pltpu.VMEM((offsets, rows), jnp.int32),
            pltpu.VMEM((offsets, chans, chans), BF16),
            pltpu.VMEM((offsets, chans, chans), BF16),
            pltpu.VMEM((chans, wide), BF16),
            pltpu.VMEM((chans, wide), BF16),
            pltpu.VMEM((chans, wide), BF16),
            pltpu.VMEM((chans, ext), BF16),
            pltpu.VMEM((chans, ext), BF16),
            pltpu.VMEM((chans, ext), BF16),
            pltpu.VMEM((chans, rows), BF16),
            pltpu.VMEM((offsets, ext), F32),
            pltpu.VMEM((wide, rows), BF16),
            pltpu.VMEM((wide, rows), BF16),
            pltpu.VMEM((chans, rows), F32),
            pltpu.VMEM((2, HALO, chans), BF16),
            pltpu.VMEM((2, HALO, chans), BF16),
            pltpu.VMEM((2, offsets, HALO), jnp.int32),
            pltpu.VMEM((2, chans, HALO), BF16),
            pltpu.VMEM((2, chans, HALO), BF16),
            pltpu.SemaphoreType.DMA((6,)),
            pltpu.SemaphoreType.DMA((4, 2)),
            pltpu.SemaphoreType.DMA((4, 2)),
            pltpu.SemaphoreType.DMA((2, len(cuts) - 1)),
            pltpu.VMEM((2, part_rows, chans), F32),
            pltpu.VMEM((2, part_rows, chans), BF16),
            pltpu.VMEM((2, piece, chans), BF16),
            pltpu.VMEM((2, half, chans), BF16),
            pltpu.VMEM((2, half, chans), F32),
            pltpu.VMEM((2, group - 1, piece, chans), BF16),
            pltpu.VMEM((2, far, piece, chans), BF16),
        ] + [pltpu.SemaphoreType.DMA((2, len(cuts) - 1, count))] * 4,
        compiler_params=pltpu.CompilerParams(
            collective_id=0, has_side_effects=True, vmem_limit_bytes=64000000),
    )(features, grad_out, w1, w2, rulebook, live_blocks)


def grouping(region, block):
    depth = block // 2
    near = 2 if depth % 2 == 0 else 1
    return region // 2 * 2, near, depth // near


def sum_stages(region, block, scale, cuts, wide, part, total, outs, store, held, sent, got1,
               got2, got3, there, back):
    planes, near, far = grouping(region, block)
    group = planes * near
    r, b = lax.axis_index("region"), lax.axis_index("block")
    c, y, x, z = lax.rem(r, 2), r // 2, lax.rem(b, 2), b // 2
    q = (y * 2 + x) * near + lax.rem(z, near)
    f = z // near

    def device(core, member, away):
        plane = member // near
        deep = away * near + lax.rem(member, near)
        return {"region": plane // 2 * 2 + core, "block": deep * 2 + lax.rem(plane, 2)}

    partner = device(1 - c, q, f)
    near_peers = [device(c, lax.rem(q + d, group), f) for d in range(1, group)]
    far_peers = [device(c, q, lax.rem(f + d, far)) for d in range(1, far)]

    def stages(i, n):
        base, size = cuts[n], cuts[n + 1] - cuts[n]
        half = size // 2
        piece = half // group
        base_half = base // 2
        base_piece = base_half // group

        def at(start, index, count):
            return pl.ds(pl.multiple_of(start + index * count, 16), count)

        def remote(src, dst, sems, m, peer):
            copy = pltpu.make_async_remote_copy(
                src_ref=src, dst_ref=dst, send_sem=sems[0].at[i, n, m],
                recv_sem=sems[1].at[i, n, m], device_id=peer, device_id_type=MESH)
            copy.start()
            return copy

        halves, pieces = pl.ds(base_half, half), pl.ds(base_piece, piece)

        first = remote(part.at[i, at(base, 1 - c, half)], got1.at[i, halves], there, 0, partner)
        yield
        first.wait()
        second = []
        for d in range(1, group):
            to = lax.rem(q + d, group)
            theirs = at(base_half, to, piece)
            sent[i, theirs] = (part[i, at(base, c * group + to, piece)]
                               + got1[i, theirs]).astype(BF16)
            second.append(remote(sent.at[i, theirs], got2.at[i, d - 1, pieces], there, d,
                                 near_peers[d - 1]))
        yield
        value = part[i, at(base, c * group + q, piece)] + got1[i, at(base_half, q, piece)]
        for d in range(1, group):
            second[d - 1].wait()
            value = value + got2[i, d - 1, pieces].astype(F32)
        held[i, pieces] = value.astype(BF16)
        got3[i, 0, pieces] = held[i, pieces]
        third = [remote(held.at[i, pieces], got3.at[i, d, pieces], there, group - 1 + d,
                        far_peers[d - 1])
                 for d in range(1, far)]
        yield
        for copy in third:
            copy.wait()
        value = jnp.zeros((piece, part.shape[2]), F32)
        for d in range(far):
            value = value + got3[i, lax.rem(f + far - d, far), pieces].astype(F32)
        place = at(base, c * group + q, piece)
        total[i, place] = (value / scale).astype(BF16)
        for where, peers, sem in (
            (place, near_peers, 1),
            (at(base, c, half), [partner], 0),
        ):
            moved = [remote(total.at[i, where], total.at[i, where], back, sem + m, peer)
                     for m, peer in enumerate(peers)]
            yield
            for copy in moved:
                copy.wait()
        kept = pl.ds(base, min(size, wide - base))
        copy = pltpu.make_async_copy(total.at[i, kept], outs[i].at[kept], store.at[i, n])
        copy.start()
        yield copy

    return stages, [partner] + near_peers + far_peers


def widen_kernel(a, b, c, a_out, b_out, c_out, kept, narrow, wide, loaded, stored, through):
    count = loaded.shape[1]
    rows = b.shape[0] // count
    inward = pltpu.make_async_copy(a, kept, through.at[0])
    outward = pltpu.make_async_copy(kept, a_out, through.at[1])
    pieces = [(i, n, pl.ds(n * rows, rows)) for i in range(2) for n in range(count)]
    loads = [pltpu.make_async_copy((b, c)[i].at[at], narrow.at[i, at], loaded.at[i, n])
             for i, n, at in pieces]
    stores = [pltpu.make_async_copy(wide.at[i, at], (b_out, c_out)[i].at[at], stored.at[i, n])
              for i, n, at in pieces]
    for copy in loads:
        copy.start()
    inward.start()
    for (i, n, at), load, store in zip(pieces, loads, stores):
        load.wait()
        wide[i, at] = narrow[i, at].astype(F32)
        store.start()
    inward.wait()
    outward.start()
    for copy in stores:
        copy.wait()
    outward.wait()


def widen(grad_in, part1, part2):
    rows, chans = grad_in.shape
    wide = part1.shape[0]
    steps = STEPS if wide % (16 * STEPS) == 0 else 1
    hbm = pl.BlockSpec(memory_space=pl.ANY)
    return pl.pallas_call(
        widen_kernel,
        out_shape=(
            jax.ShapeDtypeStruct((rows, chans), BF16),
            jax.ShapeDtypeStruct((wide, chans), F32),
            jax.ShapeDtypeStruct((wide, chans), F32),
        ),
        in_specs=[hbm] * 3,
        out_specs=(hbm,) * 3,
        scratch_shapes=[
            pltpu.VMEM((rows, chans), BF16),
            pltpu.VMEM((2, wide, chans), BF16),
            pltpu.VMEM((2, wide, chans), F32),
            pltpu.SemaphoreType.DMA((2, steps)),
            pltpu.SemaphoreType.DMA((2, steps)),
            pltpu.SemaphoreType.DMA((2,)),
        ],
        compiler_params=pltpu.CompilerParams(vmem_limit_bytes=64000000),
    )(grad_in, part1, part2)


def on_device(features, grad_out, w1, w2, rulebook, live_blocks):
    offsets, chans = w1.shape[0], w1.shape[1]
    region, block = lax.axis_size("region"), lax.axis_size("block")
    planes, near, far = grouping(region, block)
    step = 32 * planes * near
    units = (offsets * chans + step - 1) // step
    cuts = sorted({units * share // SHARES[-1] * step for share in SHARES})
    scale = float(features.shape[0] * region * block) ** 0.5
    grad_in, *both = slab_step(
        features, grad_out, w1, w2, rulebook, live_blocks, cuts, scale)
    grad_in, grad_w1, grad_w2 = widen(grad_in, *both)
    return (grad_in, grad_w1.reshape(w1.shape), grad_w2.reshape(w2.shape))


def solution(mesh):
    return jax.shard_map(
        on_device,
        mesh=mesh,
        in_specs=(
            P(("region", "block"), None),
            P(("region", "block"), None),
            P(),
            P(),
            P(None, ("region", "block")),
            P(("region", "block")),
        ),
        out_specs=(P(("region", "block"), None), P(), P()),
        check_vma=False,
    )
```
